256 devices in a mesh: dp: 64 (over x, z, core), rep: 4 (over y).
Axes of the slice: x: 4, y: 4, z: 8, core: 2. Of those that a mesh axis runs over, the one named last changes fastest.
Arguments:
- tokens: bfloat16 [524288, 1280], P(('dp', 'rep')), may hold values from -24 to 24
- sketch_map: bfloat16 [524288, 128], P(('dp', 'rep')), may hold values from -0.125 to 0.125
- test_matrix: bfloat16 [4, 8192, 128], P('rep'), may hold values from -0.03125 to 0.03125
Outputs:
- basis: float32 [1280, 128], P('dp')
- factor: float32 [128, 128], replicated
The draws below stay inside these ranges and needn't reach their ends.
All inputs are finite; a program needn't handle non-finite values.
Results may differ from the reference program's by a relative error of at most 0.0051.
Values may be sent and summed in bfloat16 or wider, within the bound.
No kernel may reach another device: no remote copies, remote signals or barrier semaphores. Data moves between devices by JAX's collectives and lax.ppermute only.
A program may use at most 64 MiB of HBM per device.

```python
import jax
import jax.numpy as jnp
from jax import lax

D = 1280
K = 128
ITERS = 2
TOK_DEV = 2048
TOKENS = 524288
SKETCH_ROWS = 8192
N_DP = 64
N_REP = 4


def raised(entries, rng, source, target, blocks, factor):
    owner, partner = [(jnp.arange(entries.shape[dim]) // (entries.shape[dim] // blocks)).reshape([-1 if axis == dim else 1 for axis in range(entries.ndim)]) for dim in (source, target)]
    chosen = jax.random.permutation(rng, blocks)[partner]
    strong = (owner == chosen) | (owner == (partner + blocks // 2) % blocks)
    return jnp.where(strong, factor * entries, entries)


def levels(stream_key, extent, pieces, least, largest):
    factor_of = 1.0
    for position, blocks in pieces:
        draws = jax.random.uniform(jax.random.fold_in(jax.random.fold_in(stream_key, 6), position), (blocks,), jnp.float32, least / len(pieces), largest / len(pieces))
        factor_of = factor_of * jnp.repeat(jnp.exp(draws), extent[position] // blocks).reshape((-1,) + (1,) * (len(extent) - 1 - position))
    return factor_of


def centred(rng, dims, scale, limit, split=(), kind=jnp.bfloat16):
    values = jax.random.normal(rng, dims, jnp.float32) * scale
    if len(split) > 0:
        values = levels(rng, dims, split, -0.22, 0.18) * values
    return jnp.clip(values, min=-limit, max=limit).astype(kind)


def bell_draw_with(key, shape, width, most, pieces, heavy, kind=jnp.bfloat16):
    array = width * jax.random.normal(key, shape, jnp.float32)
    if pieces:
        array = array * levels(key, shape, pieces, -0.22, 0.18)
    return jnp.clip(raised(array, jax.random.fold_in(key, 3), *heavy), -most, most).astype(kind)


def setup_inputs(seed: int = 0) -> dict:
    key_list = jax.random.split(jax.random.key(seed), 4)
    tokens = bell_draw_with(key_list[0], (TOKENS, D), 1.0, 24.0, ((0, 256),), (0, 1, 256, 6.0))
    sketch_map = centred(key_list[1], (TOKENS, K), TOK_DEV ** -0.5, 0.125, ((0, 256),))
    test_matrix = centred(key_list[2], (N_REP, SKETCH_ROWS, K), (SKETCH_ROWS * N_REP) ** -0.5, 0.03125, ((0, 4),))
    return dict(tokens=tokens, sketch_map=sketch_map, test_matrix=test_matrix)


def orthonormal(matrix):
    gram = jnp.dot(matrix.T.astype(jnp.float32), matrix.astype(jnp.float32), precision=lax.Precision.HIGHEST, preferred_element_type=jnp.float32)
    lower = jnp.linalg.cholesky(gram)
    basis = jax.scipy.linalg.solve_triangular(lower, matrix.T, lower=True).T
    return (basis, lower.T)

def reference(tokens, sketch_map, test_matrix):
    devices = N_DP * N_REP
    slabs = tokens.reshape(devices, TOK_DEV, D)
    maps = sketch_map.reshape(devices, TOK_DEV, K)

    def one_sketch(pair):
        return lax.dot_general(pair[1].astype(jnp.float32), pair[0].astype(jnp.float32), (((0,), (0,)), ((), ())), preferred_element_type=jnp.float32).astype(jnp.bfloat16)
    sketches = lax.map(one_sketch, (slabs, maps))
    grouped = sketches.reshape(N_DP, N_REP, K, D).transpose(1, 0, 2, 3).reshape(N_REP, N_DP * K, D)
    start = jnp.zeros((D, K), jnp.float32)
    for group in range(N_REP):
        start = start + lax.dot_general(grouped[group].astype(jnp.float32), test_matrix[group].astype(jnp.float32), (((0,), (0,)), ((), ())), preferred_element_type=jnp.float32)
    current, factor = orthonormal(start)
    for step in range(ITERS):
        rounded = current.astype(jnp.bfloat16)
        projected = jnp.dot(tokens.astype(jnp.float32), rounded.astype(jnp.float32), preferred_element_type=jnp.float32).astype(jnp.bfloat16)
        summed = lax.dot_general(tokens.astype(jnp.float32), projected.astype(jnp.float32), (((0,), (0,)), ((), ())), preferred_element_type=jnp.float32)
        current, factor = orthonormal(summed / TOKENS)
    return (current, factor)
```

```python
import jax
import jax.numpy as jnp
from jax import lax
from jax.experimental import pallas as pl
from jax.experimental.pallas import tpu as pltpu
from jax.sharding import Mesh
from jax.sharding import PartitionSpec as P

ITERS = 2
ALL = ("x", "z", "c", "y")
LANES = 128
SUB = 8
VMEM_LIMIT = 60 * 1024 * 1024
F32 = jnp.float32
BF16 = jnp.bfloat16
HI = lax.Precision.HIGHEST
NN = (((1,), (0,)), ((), ()))
NT = (((1,), (1,)), ((), ()))


def layout(width):
    n = width // LANES
    index = {}
    for i in range(n):
        for j in range(i, n):
            index[i, j] = n + len(index)
    used = n + len(index)
    total = used + used % 2
    return n, index, used, total


def local_products(width, tokens_dev):
    n, index, used, total = layout(width)
    wide = 2 * LANES
    rows = total * LANES // 2

    def kernel(core, tok, smap, test, keep, send, xt, acc, sem):
        for i in range(n):
            cols = slice(i * LANES, (i + 1) * LANES)
            xt[cols, :] = tok[:, cols].T
        sketch = jnp.dot(smap[...].T, tok[...], preferred_element_type=F32).astype(BF16)
        start = jnp.dot(test[...].T, sketch, preferred_element_type=F32)
        for i in range(n):
            acc[i * LANES : (i + 1) * LANES, :] = start[:, i * LANES : (i + 1) * LANES]
        for b in range(used, total):
            acc[b * LANES : (b + 1) * LANES, :] = jnp.zeros((LANES, LANES), F32)
        for big in range(n // 2):
            high = (big + 1) * wide
            out = jnp.dot(
                xt[:high, :], tok[:, big * wide : high], preferred_element_type=F32
            )
            for j in range(2):
                col = 2 * big + j
                for i in range(col + 1):
                    at = index[i, col] * LANES
                    acc[at : at + LANES, :] = out[
                        i * LANES : (i + 1) * LANES, j * LANES : (j + 1) * LANES
                    ]
        c = core[0]
        first = pltpu.make_async_copy(acc.at[pl.ds((1 - c) * rows, rows)], send, sem.at[0])
        second = pltpu.make_async_copy(acc.at[pl.ds(c * rows, rows)], keep, sem.at[1])
        first.start()
        second.start()
        first.wait()
        second.wait()

    half = jax.ShapeDtypeStruct((rows, LANES), F32)
    return pl.pallas_call(
        kernel,
        out_shape=(half, half),
        in_specs=[
            pl.BlockSpec(memory_space=pltpu.SMEM),
            pl.BlockSpec(memory_space=pltpu.VMEM),
            pl.BlockSpec(memory_space=pltpu.VMEM),
            pl.BlockSpec(memory_space=pltpu.VMEM),
        ],
        out_specs=[pl.BlockSpec(memory_space=pl.ANY), pl.BlockSpec(memory_space=pl.ANY)],
        scratch_shapes=[
            pltpu.VMEM((width, tokens_dev), BF16),
            pltpu.VMEM((total * LANES, LANES), F32),
            pltpu.SemaphoreType.DMA((2,)),
        ],
        compiler_params=pltpu.CompilerParams(vmem_limit_bytes=VMEM_LIMIT),
        name="local_products",
    )


def eliminate(gram):
    k = gram.shape[0]
    blocks = k // SUB
    lane = lax.broadcasted_iota(jnp.int32, (SUB, k), 1)
    row = lax.broadcasted_iota(jnp.int32, (SUB, k), 0)
    work = []
    for b in range(blocks):
        eye = jnp.where(lane == row + b * SUB, 1.0, 0.0).astype(F32)
        work.append((gram[b * SUB : (b + 1) * SUB, :], eye))
    factor, inverse = [], []
    for b in range(blocks):
        a, e = work[b]
        at = b * SUB
        d = {}
        for p in range(SUB):
            for q in range(p, SUB):
                d[p, q] = jnp.broadcast_to(a[p : p + 1, at + q : at + q + 1], (1, k))
        ra = [a[p : p + 1, :] for p in range(SUB)]
        re = [e[p : p + 1, :] for p in range(SUB)]
        for p in range(SUB):
            pivot = d[p, p]
            y = lax.rsqrt(pivot)
            y = y * (1.5 - 0.5 * pivot * y * y)
            for q in range(p + 1, SUB):
                d[p, q] = d[p, q] * y
            ra[p] = ra[p] * y
            re[p] = re[p] * y
            for q in range(p + 1, SUB):
                for s in range(q, SUB):
                    d[q, s] = d[q, s] - d[p, q] * d[p, s]
                ra[q] = ra[q] - d[p, q] * ra[p]
                re[q] = re[q] - d[p, q] * re[p]
        fa = jnp.concatenate(ra, axis=0)
        fe = jnp.concatenate(re, axis=0)
        factor.append(jnp.where(lane >= row + at, fa, 0.0))
        inverse.append(fe)
        if b + 1 < blocks:
            turned = fa.T
            for o in range(b + 1, blocks):
                wa, we = work[o]
                cols = turned[o * SUB : (o + 1) * SUB, :]
                for p in range(SUB):
                    coef = jnp.broadcast_to(cols[:, p : p + 1], (SUB, k))
                    wa = wa - coef * ra[p]
                    we = we - coef * re[p]
                work[o] = (wa, we)
    return jnp.concatenate(factor, axis=0), jnp.concatenate(inverse, axis=0)


def refine(width, k, strip, total_tokens):
    n, index, used, total = layout(width)
    rows = total * LANES // 2

    def orthonormal(pt):
        gram = lax.dot_general(pt, pt, NT, precision=HI, preferred_element_type=F32)
        factor, inverse = eliminate(gram)
        return jnp.dot(inverse, pt, precision=HI, preferred_element_type=F32), factor

    def kernel(where, mine, other, basis, factor_out, acc, parts, zt, turned, sem):
        c = where[0]
        first = pltpu.make_async_copy(mine, acc.at[pl.ds(c * rows, rows)], sem.at[0])
        second = pltpu.make_async_copy(other, acc.at[pl.ds((1 - c) * rows, rows)], sem.at[1])
        first.start()
        second.start()
        first.wait()
        second.wait()
        for (i, j), b in index.items():
            v = acc[b * LANES : (b + 1) * LANES, :]
            hi = v.astype(BF16)
            rest = v - hi.astype(F32)
            mid = rest.astype(BF16)
            low = (rest - mid.astype(F32)).astype(BF16)
            ri = slice(i * LANES, (i + 1) * LANES)
            rj = slice(j * LANES, (j + 1) * LANES)
            parts[0, ri, rj] = hi
            parts[1, ri, rj] = mid
            parts[2, ri, rj] = low
        pt = jnp.concatenate([acc[i * LANES : (i + 1) * LANES, :] for i in range(n)], axis=1)
        vt, factor = orthonormal(pt)
        for _ in range(ITERS):
            vb = vt.astype(BF16)
            for j in range(n):
                high = (j + 1) * LANES
                rj = slice(j * LANES, high)
                z = jnp.zeros((k, LANES), F32)
                for s in (2, 1, 0):
                    z = z + lax.dot_general(
                        vb[:, :high], parts[s, :high, rj], NN, preferred_element_type=F32
                    )
                    if j + 1 < n:
                        z = z + lax.dot_general(
                            vb[:, high:], parts[s, rj, high:], NT, preferred_element_type=F32
                        )
                zt[:, rj] = z * (1.0 / total_tokens)
            vt, factor = orthonormal(zt[...])
        factor_out[...] = factor
        for i in range(n):
            cols = slice(i * LANES, (i + 1) * LANES)
            turned[cols, :] = vt[:, cols].T
        basis[...] = turned[pl.ds(where[1] * strip, strip), :]

    return pl.pallas_call(
        kernel,
        out_shape=(
            jax.ShapeDtypeStruct((strip, k), F32),
            jax.ShapeDtypeStruct((k, k), F32),
        ),
        in_specs=[
            pl.BlockSpec(memory_space=pltpu.SMEM),
            pl.BlockSpec(memory_space=pl.ANY),
            pl.BlockSpec(memory_space=pl.ANY),
        ],
        out_specs=[
            pl.BlockSpec(memory_space=pltpu.VMEM),
            pl.BlockSpec(memory_space=pltpu.VMEM),
        ],
        scratch_shapes=[
            pltpu.VMEM((total * LANES, LANES), F32),
            pltpu.VMEM((3, width, width), BF16),
            pltpu.VMEM((k, width), F32),
            pltpu.VMEM((width, k), F32),
            pltpu.SemaphoreType.DMA((2,)),
        ],
        compiler_params=pltpu.CompilerParams(vmem_limit_bytes=VMEM_LIMIT),
        name="refine",
    )


def body(tokens, sketch_map, test_matrix):
    tokens_dev, width = tokens.shape
    k = sketch_map.shape[1]
    strip = width // lax.axis_size(("x", "z", "c"))
    total_tokens = tokens_dev * lax.axis_size(ALL)
    core = lax.axis_index("c")
    slab = lax.axis_index(("x", "z", "c"))
    test = lax.dynamic_slice_in_dim(test_matrix[0], slab * k, k, 0)
    with jax.named_scope("products"):
        keep, send = local_products(width, tokens_dev)(
            core.reshape(1), tokens, sketch_map, test
        )
    rows = keep.shape[0]
    swap = [(0, 1), (1, 0)]
    with jax.named_scope("over_core"):
        half = keep + lax.ppermute(send, "c", swap)
    with jax.named_scope("over_xy"):
        plane = lax.axis_size(("x", "y"))
        tiles = half.reshape(plane, rows // plane, LANES)
        piece = jnp.sum(lax.all_to_all(tiles, ("x", "y"), 0, 0, tiled=True), axis=0)
    with jax.named_scope("over_z"):
        copies = jnp.broadcast_to(piece, (lax.axis_size("z"), *piece.shape))
        piece = jnp.sum(lax.all_to_all(copies, "z", 0, 0, tiled=True), axis=0)
    with jax.named_scope("back_xy"):
        copies = jnp.broadcast_to(piece, (plane, *piece.shape))
        half = lax.all_to_all(copies, ("x", "y"), 0, 0, tiled=True).reshape(rows, LANES)
    with jax.named_scope("back_core"):
        other = lax.ppermute(half, "c", swap)
    with jax.named_scope("refine"):
        where = jnp.stack([core, slab])
        return refine(width, k, strip, total_tokens)(where, half, other)


def solution(mesh):
    finer = Mesh(mesh.devices.reshape(4, 8, 2, mesh.shape["rep"]), ALL)
    return jax.shard_map(
        body,
        mesh=finer,
        in_specs=(P(ALL, None), P(ALL, None), P("y", None, None)),
        out_specs=(P(("x", "z", "c"), None), P()),
        check_vma=False,
    )
```

```python
import jax
import jax.numpy as jnp
from jax import lax
from jax.experimental import pallas as pl
from jax.experimental.pallas import tpu as pltpu
from jax.sharding import Mesh
from jax.sharding import PartitionSpec as P

ITERS = 2
ALL = ("x", "z", "c", "y")
LANES = 128
SUB = 8
MIB = 1024 * 1024
F32 = jnp.float32
BF16 = jnp.bfloat16
HI = lax.Precision.HIGHEST
NN = (((1,), (0,)), ((), ()))
NT = (((1,), (1,)), ((), ()))
TN = (((0,), (0,)), ((), ()))


class Packing:
    def __init__(self, width, pieces):
        self.n = width // LANES
        self.pairs = self.n // 2
        self.diagonals = 0
        start_at = -(-self.pairs // SUB) * SUB
        covariance = self.pairs * (2 * self.pairs - 1) + self.pairs
        bare = start_at + (self.n + covariance) * LANES
        self.rows = -(-bare // (pieces * SUB)) * (pieces * SUB)
        at = self.rows - (self.n + covariance) * LANES
        self.start = at
        at += self.n * LANES
        self.start_end = at
        self.offset = {}
        self.group = {}
        for pair in reversed(range(self.pairs)):
            begin = at
            left, right = 2 * pair, 2 * pair + 1
            for j in (left, right):
                for i in range(j):
                    self.offset[i, j] = at
                    at += LANES
            self.offset[left, left] = at
            at += LANES
            self.group[pair] = (begin, at)
        self.half = self.rows // 2

    def runs(self, begin, end):
        cuts = [begin] + ([self.half] if begin < self.half < end else []) + [end]
        return list(zip(cuts[:-1], cuts[1:]))


def local_products(pack, width, tokens_dev, k):
    chunks = 2
    part = tokens_dev // chunks
    runs = pack.runs(0, pack.start_end)
    for pair in reversed(range(pack.pairs)):
        runs += pack.runs(*pack.group[pair])

    def kernel(tok_hbm, smap_hbm, test_hbm, keep, send, tok, smap, test, acc, sem, out_sem):
        core = lax.axis_index("c")
        slab = lax.axis_index(("x", "z", "c"))
        loads = []
        for s in range(chunks):
            rows = pl.ds(s * part, part)
            loads.append(pltpu.make_async_copy(tok_hbm.at[rows], tok.at[rows], sem.at[s]))
        load_map = pltpu.make_async_copy(smap_hbm, smap, sem.at[chunks])
        load_test = pltpu.make_async_copy(
            test_hbm.at[0, pl.ds(pl.multiple_of(slab * k, k), k)], test, sem.at[chunks + 1]
        )
        load_map.start()
        for load in loads:
            load.start()
        load_test.start()

        def copies(home, first, last):
            made = []
            for r, (begin, end) in enumerate(runs):
                if begin < first or end > last:
                    continue
                side = begin // pack.half
                to = keep if side == home else send
                made.append(
                    pltpu.make_async_copy(
                        acc.at[begin:end],
                        to.at[begin - side * pack.half : end - side * pack.half],
                        out_sem.at[r],
                    )
                )
            return made

        def store(begin, end):
            for home in range(2):

                @pl.when(core == home)
                def _():
                    for copy in copies(home, begin, end):
                        copy.start()

        load_map.wait()
        sketch = jnp.zeros((k, width), F32)
        for s in range(chunks):
            loads[s].wait()
            rows = slice(s * part, (s + 1) * part)
            sketch = sketch + lax.dot_general(
                smap[rows, :], tok[rows, :], TN, preferred_element_type=F32
            )
        load_test.wait()
        start = lax.dot_general(test[...], sketch.astype(BF16), TN, preferred_element_type=F32)
        acc[: pack.start, :] = jnp.zeros((pack.start, LANES), F32)
        for i in range(pack.n):
            at = pack.start + i * LANES
            acc[at : at + LANES, :] = start[:, i * LANES : (i + 1) * LANES]
        row = lax.broadcasted_iota(jnp.int32, (LANES, LANES), 0)
        col = lax.broadcasted_iota(jnp.int32, (LANES, LANES), 1)
        for pair in reversed(range(pack.pairs)):
            base = 2 * pair * LANES
            high = base + 2 * LANES
            out = lax.dot_general(
                tok[:, :high], tok[:, base:high], TN, preferred_element_type=F32
            )
            for j in range(2):
                for i in range(2 * pair + j):
                    at = pack.offset[i, 2 * pair + j]
                    acc[at : at + LANES, :] = out[
                        i * LANES : (i + 1) * LANES, j * LANES : (j + 1) * LANES
                    ]
            upper = out[base : base + LANES, :LANES]
            lower = out[base + LANES : high, LANES:]
            at = pack.offset[2 * pair, 2 * pair]
            acc[at : at + LANES, :] = jnp.where(row <= col, upper, lower)
            acc[pair : pair + 1, :] = jnp.sum(jnp.where(row == col, lower, 0.0), axis=0)[None, :]
            store(*pack.group[pair])
        store(0, pack.start_end)
        for home in range(2):

            @pl.when(core == home)
            def _():
                for copy in copies(home, 0, pack.rows):
                    copy.wait()

    half = jax.ShapeDtypeStruct((pack.half, LANES), F32)
    return pl.pallas_call(
        kernel,
        out_shape=(half, half),
        in_specs=[pl.BlockSpec(memory_space=pl.ANY)] * 3,
        out_specs=[pl.BlockSpec(memory_space=pl.ANY)] * 2,
        scratch_shapes=[
            pltpu.VMEM((tokens_dev, width), BF16),
            pltpu.VMEM((tokens_dev, k), BF16),
            pltpu.VMEM((k, k), BF16),
            pltpu.VMEM((pack.rows, LANES), F32),
            pltpu.SemaphoreType.DMA((chunks + 2,)),
            pltpu.SemaphoreType.DMA((len(runs),)),
        ],
        compiler_params=pltpu.CompilerParams(vmem_limit_bytes=24 * MIB),
        name="local_products",
    )


def eliminate(gram):
    k = gram.shape[0]
    blocks = k // SUB
    lane = lax.broadcasted_iota(jnp.int32, (SUB, k), 1)
    row = lax.broadcasted_iota(jnp.int32, (SUB, k), 0)
    work, trace = [], []
    for b in range(blocks):
        work.append(gram[b * SUB : (b + 1) * SUB, :])
        trace.append(jnp.where(lane == row + b * SUB, 1.0, 0.0).astype(F32))
    factor, inverse = [], []
    for b in range(blocks):
        at = b * SUB
        spread = {}
        for o in range(b, blocks):
            for q in range(SUB):
                spread[o, q] = jnp.broadcast_to(work[o][:, at + q : at + q + 1], (SUB, k))
        d = {(p, q): spread[b, q][p : p + 1, :] for p in range(SUB) for q in range(p, SUB)}
        scale = []
        for p in range(SUB):
            scale.append(lax.rsqrt(d[p, p]))
            for q in range(p + 1, SUB):
                d[p, q] = d[p, q] * scale[p]
            for q in range(p + 1, SUB):
                for s in range(q, SUB):
                    d[q, s] = d[q, s] - d[p, q] * d[p, s]
        ra = [work[b][p : p + 1, :] for p in range(SUB)]
        re = [trace[b][p : p + 1, :] for p in range(SUB)]
        for p in range(SUB):
            ra[p] = ra[p] * scale[p]
            re[p] = re[p] * scale[p]
            for q in range(p + 1, SUB):
                ra[q] = ra[q] - d[p, q] * ra[p]
                re[q] = re[q] - d[p, q] * re[p]
        for o in range(b + 1, blocks):
            column = [spread[o, q] for q in range(SUB)]
            for p in range(SUB):
                column[p] = column[p] * scale[p]
                for q in range(p + 1, SUB):
                    column[q] = column[q] - d[p, q] * column[p]
                work[o] = work[o] - column[p] * ra[p]
                trace[o] = trace[o] - column[p] * re[p]
        factor.append(jnp.where(lane >= row + at, jnp.concatenate(ra, axis=0), 0.0))
        inverse.append(jnp.concatenate(re, axis=0))
    return jnp.concatenate(factor, axis=0), jnp.concatenate(inverse, axis=0)


def refine(pack, width, k, strip, total_tokens):
    n = pack.n

    def orthonormal(pt):
        gram = lax.dot_general(pt, pt, NT, precision=HI, preferred_element_type=F32)
        factor, inverse = eliminate(gram)
        return jnp.dot(inverse, pt, precision=HI, preferred_element_type=F32), factor

    def kernel(mine, other, basis, factor_out, acc, parts, zt, turned, sem):
        core = lax.axis_index("c")
        slab = lax.axis_index(("x", "z", "c"))
        cut = pack.start_end

        def load(home, run):
            sides = (mine, other) if home == 0 else (other, mine)
            side, begin, end = ((0, 0, cut), (0, cut, pack.half), (1, 0, pack.half))[run]
            at = side * pack.half
            return pltpu.make_async_copy(
                sides[side].at[begin:end], acc.at[at + begin : at + end], sem.at[run]
            )

        def each_home(action):
            for home in range(2):

                @pl.when(core == home)
                def _():
                    action(home)

        each_home(lambda home: [load(home, run).start() for run in range(3)])
        each_home(lambda home: load(home, 0).wait())
        pt = jnp.concatenate(
            [acc[pack.start + i * LANES : pack.start + (i + 1) * LANES, :] for i in range(n)],
            axis=1,
        )
        vt, factor = orthonormal(pt)
        each_home(lambda home: [load(home, run).wait() for run in (1, 2)])

        def put(i, j, v):
            hi = v.astype(BF16)
            rest = v - hi.astype(F32)
            mid = rest.astype(BF16)
            low = (rest - mid.astype(F32)).astype(BF16)
            ri = slice(i * LANES, (i + 1) * LANES)
            rj = slice(j * LANES, (j + 1) * LANES)
            parts[0, ri, rj] = hi
            parts[1, ri, rj] = mid
            parts[2, ri, rj] = low

        row = lax.broadcasted_iota(jnp.int32, (LANES, LANES), 0)
        col = lax.broadcasted_iota(jnp.int32, (LANES, LANES), 1)
        for (i, j), at in pack.offset.items():
            v = acc[at : at + LANES, :]
            if i < j:
                put(i, j, v)
            else:
                flipped = v.T
                put(i, i, jnp.where(row <= col, v, flipped))
                pair = i // 2
                whole = jnp.where(row > col, v, flipped)
                put(i + 1, i + 1, jnp.where(row == col, acc[pair : pair + 1, :], whole))
        for _ in range(ITERS):
            vb = vt.astype(BF16)
            for j in range(n):
                high = (j + 1) * LANES
                rj = slice(j * LANES, high)
                z = jnp.zeros((k, LANES), F32)
                for s in (2, 1, 0):
                    z = z + lax.dot_general(
                        vb[:, :high], parts[s, :high, rj], NN, preferred_element_type=F32
                    )
                    if j + 1 < n:
                        z = z + lax.dot_general(
                            vb[:, high:], parts[s, rj, high:], NT, preferred_element_type=F32
                        )
                zt[:, rj] = z * (1.0 / total_tokens)
            vt, factor = orthonormal(zt[...])
        factor_out[...] = factor
        for i in range(n):
            cols = slice(i * LANES, (i + 1) * LANES)
            turned[cols, :] = vt[:, cols].T
        basis[...] = turned[pl.ds(slab * strip, strip), :]

    return pl.pallas_call(
        kernel,
        out_shape=(
            jax.ShapeDtypeStruct((strip, k), F32),
            jax.ShapeDtypeStruct((k, k), F32),
        ),
        in_specs=[pl.BlockSpec(memory_space=pl.ANY)] * 2,
        out_specs=[pl.BlockSpec(memory_space=pltpu.VMEM)] * 2,
        scratch_shapes=[
            pltpu.VMEM((pack.rows, LANES), F32),
            pltpu.VMEM((3, width, width), BF16),
            pltpu.VMEM((k, width), F32),
            pltpu.VMEM((width, k), F32),
            pltpu.SemaphoreType.DMA((3,)),
        ],
        compiler_params=pltpu.CompilerParams(vmem_limit_bytes=28 * MIB),
        name="refine",
    )


def body(tokens, sketch_map, test_matrix):
    tokens_dev, width = tokens.shape
    k = sketch_map.shape[1]
    strip = width // lax.axis_size(("x", "z", "c"))
    total_tokens = tokens_dev * lax.axis_size(ALL)
    plane = lax.axis_size(("x", "y"))
    pack = Packing(width, 2 * plane)
    with jax.named_scope("products"):
        held = [
            pltpu.with_memory_space_constraint(array, pltpu.HBM)
            for array in (tokens, sketch_map, test_matrix)
        ]
        keep, send = local_products(pack, width, tokens_dev, k)(*held)
    swap = [(0, 1), (1, 0)]
    with jax.named_scope("over_core"):
        half = keep + lax.ppermute(send, "c", swap)
    with jax.named_scope("over_xy"):
        tiles = half.reshape(plane, pack.half // plane, LANES)
        piece = jnp.sum(lax.all_to_all(tiles, ("x", "y"), 0, 0, tiled=True), axis=0)
    with jax.named_scope("over_z"):
        copies = jnp.broadcast_to(piece, (lax.axis_size("z"), *piece.shape))
        piece = jnp.sum(lax.all_to_all(copies, "z", 0, 0, tiled=True), axis=0)
    with jax.named_scope("back_xy"):
        copies = jnp.broadcast_to(piece, (plane, *piece.shape))
        half = lax.all_to_all(copies, ("x", "y"), 0, 0, tiled=True).reshape(pack.half, LANES)
    with jax.named_scope("back_core"):
        other = lax.ppermute(half, "c", swap)
    with jax.named_scope("refine"):
        return refine(pack, width, k, strip, total_tokens)(half, other)


def solution(mesh):
    finer = Mesh(mesh.devices.reshape(4, 8, 2, mesh.shape["rep"]), ALL)
    return jax.shard_map(
        body,
        mesh=finer,
        in_specs=(P(ALL, None), P(ALL, None), P("y", None, None)),
        out_specs=(P(("x", "z", "c"), None), P()),
        check_vma=False,
    )
```

```python
import jax
import jax.numpy as jnp
from jax import lax
from jax.experimental import pallas as pl
from jax.experimental.pallas import tpu as pltpu
from jax.sharding import Mesh
from jax.sharding import PartitionSpec as P

ITERS = 2
ALL = ("x", "z", "c", "y")
LANES = 128
SUB = 8
MIB = 1024 * 1024
F32 = jnp.float32
BF16 = jnp.bfloat16
HI = lax.Precision.HIGHEST
NN = (((1,), (0,)), ((), ()))
NT = (((1,), (1,)), ((), ()))
TN = (((0,), (0,)), ((), ()))


class Packing:
    def __init__(self, width, pieces):
        self.n = width // LANES
        count = self.n // 2
        last = count - 1
        self.pairs = (list(range(last - 1, -1, -2)), list(range(last, -1, -2)))
        self.rows = []
        self.offset = {}
        for stream, pairs in enumerate(self.pairs):
            used = sum(4 * pair + 2 for pair in pairs) * LANES
            head = 0 if stream else -(-count // SUB) * SUB + self.n * LANES
            total = -(-(head + used) // (pieces * SUB)) * (pieces * SUB)
            at = total - used
            if not stream:
                self.start = at - self.n * LANES
                self.start_end = at
            for pair in pairs:
                left, right = 2 * pair, 2 * pair + 1
                for j in (left, right):
                    for i in range(j):
                        self.offset[i, j] = (stream, at)
                        at += LANES
                self.offset[left, left] = (stream, at)
                at += LANES
            self.rows.append(total)


def split_out(acc, keep, send, sem, rows, core):
    def copy(home, side):
        to = keep if side == home else send
        return pltpu.make_async_copy(
            acc.at[side * rows // 2 : (side + 1) * rows // 2], to, sem.at[side]
        )

    for home in range(2):

        @pl.when(core == home)
        def _():
            for side in (1 - home, home):
                copy(home, side).start()
            for side in (1 - home, home):
                copy(home, side).wait()


def local_products(pack, stream, width, tokens_dev, k):
    chunks = 4
    part = tokens_dev // chunks
    rows_out = pack.rows[stream]

    def pair_products(pack, tok, acc):
        row = lax.broadcasted_iota(jnp.int32, (LANES, LANES), 0)
        col = lax.broadcasted_iota(jnp.int32, (LANES, LANES), 1)
        for pair in pack.pairs[stream]:
            base = 2 * pair * LANES
            high = base + 2 * LANES
            out = lax.dot_general(tok[:, :high], tok[:, base:high], TN, preferred_element_type=F32)
            for j in range(2):
                for i in range(2 * pair + j):
                    at = pack.offset[i, 2 * pair + j][1]
                    acc[at : at + LANES, :] = out[
                        i * LANES : (i + 1) * LANES, j * LANES : (j + 1) * LANES
                    ]
            upper = out[base : base + LANES, :LANES]
            lower = out[base + LANES : high, LANES:]
            at = pack.offset[2 * pair, 2 * pair][1]
            acc[at : at + LANES, :] = jnp.where(row <= col, upper, lower)

    def with_start(tok_hbm, smap_hbm, test_hbm, keep, send, tok, smap, test, acc, sem, out_sem):
        core = lax.axis_index("c")
        slab = lax.axis_index(("x", "z", "c"))
        load_map = pltpu.make_async_copy(smap_hbm, smap, sem.at[chunks])
        load_test = pltpu.make_async_copy(
            test_hbm.at[0, pl.ds(pl.multiple_of(slab * k, k), k)], test, sem.at[chunks + 1]
        )
        loads = []
        for s in range(chunks):
            rows = pl.ds(s * part, part)
            loads.append(pltpu.make_async_copy(tok_hbm.at[rows], tok.at[rows], sem.at[s]))
        load_map.start()
        for load in loads:
            load.start()
        load_test.start()
        load_map.wait()
        sketch = jnp.zeros((k, width), F32)
        for s in range(chunks):
            loads[s].wait()
            rows = slice(s * part, (s + 1) * part)
            sketch = sketch + lax.dot_general(
                smap[rows, :], tok[rows, :], TN, preferred_element_type=F32
            )
        load_test.wait()
        start = lax.dot_general(test[...], sketch.astype(BF16), TN, preferred_element_type=F32)
        acc[: pack.start, :] = jnp.zeros((pack.start, LANES), F32)
        for i in range(pack.n):
            at = pack.start + i * LANES
            acc[at : at + LANES, :] = start[:, i * LANES : (i + 1) * LANES]
        pair_products(pack, tok, acc)
        row = lax.broadcasted_iota(jnp.int32, (LANES, LANES), 0)
        col = lax.broadcasted_iota(jnp.int32, (LANES, LANES), 1)
        for pair in range(pack.n // 2):
            odd = tok[:, (2 * pair + 1) * LANES : (2 * pair + 2) * LANES]
            own = lax.dot_general(odd, odd, TN, preferred_element_type=F32)
            acc[pair : pair + 1, :] = jnp.sum(jnp.where(row == col, own, 0.0), axis=0)[None, :]
        split_out(acc, keep, send, out_sem, rows_out, core)

    def without_start(tok_hbm, keep, send, tok, acc, sem, out_sem):
        core = lax.axis_index("c")
        load = pltpu.make_async_copy(tok_hbm, tok, sem.at[0])
        load.start()
        load.wait()
        pair_products(pack, tok, acc)
        split_out(acc, keep, send, out_sem, rows_out, core)

    half = jax.ShapeDtypeStruct((rows_out // 2, LANES), F32)
    small = [] if stream else [pltpu.VMEM((tokens_dev, k), BF16), pltpu.VMEM((k, k), BF16)]
    return pl.pallas_call(
        without_start if stream else with_start,
        out_shape=(half, half),
        in_specs=[pl.BlockSpec(memory_space=pl.ANY)] * (1 if stream else 3),
        out_specs=[pl.BlockSpec(memory_space=pl.ANY)] * 2,
        scratch_shapes=[
            pltpu.VMEM((tokens_dev, width), BF16),
            *small,
            pltpu.VMEM((rows_out, LANES), F32),
            pltpu.SemaphoreType.DMA((chunks + 2,)),
            pltpu.SemaphoreType.DMA((2,)),
        ],
        compiler_params=pltpu.CompilerParams(vmem_limit_bytes=24 * MIB),
        cost_estimate=pl.CostEstimate(
            flops=2 * tokens_dev * rows_out * LANES,
            bytes_accessed=2 * tokens_dev * width + 4 * rows_out * LANES,
            transcendentals=0,
        ),
        name="products_stream_%d" % stream,
    )


def eliminate(gram):
    k = gram.shape[0]
    blocks = k // SUB
    lane = lax.broadcasted_iota(jnp.int32, (SUB, k), 1)
    row = lax.broadcasted_iota(jnp.int32, (SUB, k), 0)
    work, trace = [], []
    for b in range(blocks):
        work.append(gram[b * SUB : (b + 1) * SUB, :])
        trace.append(jnp.where(lane == row + b * SUB, 1.0, 0.0).astype(F32))
    factor, inverse = [], []
    for b in range(blocks):
        at = b * SUB
        spread = {}
        for o in range(b, blocks):
            for q in range(SUB):
                spread[o, q] = jnp.broadcast_to(work[o][:, at + q : at + q + 1], (SUB, k))
        d = {(p, q): spread[b, q][p : p + 1, :] for p in range(SUB) for q in range(p, SUB)}
        scale = []
        for p in range(SUB):
            scale.append(lax.rsqrt(d[p, p]))
            for q in range(p + 1, SUB):
                d[p, q] = d[p, q] * scale[p]
            for q in range(p + 1, SUB):
                for s in range(q, SUB):
                    d[q, s] = d[q, s] - d[p, q] * d[p, s]
        ra = [work[b][p : p + 1, :] for p in range(SUB)]
        re = [trace[b][p : p + 1, :] for p in range(SUB)]
        for p in range(SUB):
            ra[p] = ra[p] * scale[p]
            re[p] = re[p] * scale[p]
            for q in range(p + 1, SUB):
                ra[q] = ra[q] - d[p, q] * ra[p]
                re[q] = re[q] - d[p, q] * re[p]
        for o in range(b + 1, blocks):
            column = [spread[o, q] for q in range(SUB)]
            for p in range(SUB):
                column[p] = column[p] * scale[p]
                for q in range(p + 1, SUB):
                    column[q] = column[q] - d[p, q] * column[p]
                work[o] = work[o] - column[p] * ra[p]
                trace[o] = trace[o] - column[p] * re[p]
        factor.append(jnp.where(lane >= row + at, jnp.concatenate(ra, axis=0), 0.0))
        inverse.append(jnp.concatenate(re, axis=0))
    return jnp.concatenate(factor, axis=0), jnp.concatenate(inverse, axis=0)


def orthonormal(pt):
    gram = lax.dot_general(pt, pt, NT, precision=HI, preferred_element_type=F32)
    factor, inverse = eliminate(gram)
    return jnp.dot(inverse, pt, precision=HI, preferred_element_type=F32), factor


def merged(mine, other, acc, sem, home, run):
    from_half = mine if home == run else other
    rows = acc.shape[0] // 2
    return pltpu.make_async_copy(from_half, acc.at[run * rows : (run + 1) * rows], sem)


def first_basis(pack, width, k):
    def kernel(mine, other, vt_out, held, sem):
        core = lax.axis_index("c")
        for home in range(2):

            @pl.when(core == home)
            def _():
                half = mine if home == 0 else other
                load = pltpu.make_async_copy(
                    half.at[pack.start : pack.start_end], held, sem
                )
                load.start()
                load.wait()

        pt = jnp.concatenate(
            [held[i * LANES : (i + 1) * LANES, :] for i in range(pack.n)], axis=1
        )
        vt_out[...] = orthonormal(pt)[0]

    return pl.pallas_call(
        kernel,
        out_shape=jax.ShapeDtypeStruct((k, width), F32),
        in_specs=[pl.BlockSpec(memory_space=pl.ANY)] * 2,
        out_specs=pl.BlockSpec(memory_space=pltpu.VMEM),
        scratch_shapes=[pltpu.VMEM((width, LANES), F32), pltpu.SemaphoreType.DMA],
        compiler_params=pltpu.CompilerParams(vmem_limit_bytes=8 * MIB),
        cost_estimate=pl.CostEstimate(
            flops=k * k * width * 400, bytes_accessed=8 * width * k, transcendentals=k
        ),
        name="first_basis",
    )


def refine(pack, width, k, strip, total_tokens):
    n = pack.n

    def kernel(mine_0, other_0, mine_1, other_1, first, basis, factor_out, acc_0, acc_1, parts, zt, turned, sem):
        core = lax.axis_index("c")
        slab = lax.axis_index(("x", "z", "c"))
        accs = (acc_0, acc_1)
        halves = ((mine_0, other_0), (mine_1, other_1))

        def each(action):
            for home in range(2):

                @pl.when(core == home)
                def _():
                    for stream in range(2):
                        for run in range(2):
                            copy = merged(
                                *halves[stream], accs[stream], sem.at[stream, run], home, run
                            )
                            action(copy)

        each(lambda copy: copy.start())
        each(lambda copy: copy.wait())

        def put(i, j, v):
            hi = v.astype(BF16)
            rest = v - hi.astype(F32)
            mid = rest.astype(BF16)
            low = (rest - mid.astype(F32)).astype(BF16)
            ri = slice(i * LANES, (i + 1) * LANES)
            rj = slice(j * LANES, (j + 1) * LANES)
            parts[0, ri, rj] = hi
            parts[1, ri, rj] = mid
            parts[2, ri, rj] = low

        row = lax.broadcasted_iota(jnp.int32, (LANES, LANES), 0)
        col = lax.broadcasted_iota(jnp.int32, (LANES, LANES), 1)
        for (i, j), (stream, at) in pack.offset.items():
            v = accs[stream][at : at + LANES, :]
            if i < j:
                put(i, j, v)
            else:
                flipped = v.T
                put(i, i, jnp.where(row <= col, v, flipped))
                pair = i // 2
                whole = jnp.where(row > col, v, flipped)
                put(i + 1, i + 1, jnp.where(row == col, acc_0[pair : pair + 1, :], whole))
        vt = first[...]
        for _ in range(ITERS):
            vb = vt.astype(BF16)
            for j in range(n):
                high = (j + 1) * LANES
                rj = slice(j * LANES, high)
                z = jnp.zeros((k, LANES), F32)
                for s in (2, 1, 0):
                    z = z + lax.dot_general(
                        vb[:, :high], parts[s, :high, rj], NN, preferred_element_type=F32
                    )
                    if j + 1 < n:
                        z = z + lax.dot_general(
                            vb[:, high:], parts[s, rj, high:], NT, preferred_element_type=F32
                        )
                zt[:, rj] = z * (1.0 / total_tokens)
            vt, factor = orthonormal(zt[...])
        factor_out[...] = factor
        for i in range(n):
            cols = slice(i * LANES, (i + 1) * LANES)
            turned[cols, :] = vt[:, cols].T
        basis[...] = turned[pl.ds(slab * strip, strip), :]

    return pl.pallas_call(
        kernel,
        out_shape=(
            jax.ShapeDtypeStruct((strip, k), F32),
            jax.ShapeDtypeStruct((k, k), F32),
        ),
        in_specs=[pl.BlockSpec(memory_space=pl.ANY)] * 4 + [pl.BlockSpec(memory_space=pltpu.VMEM)],
        out_specs=[pl.BlockSpec(memory_space=pltpu.VMEM)] * 2,
        scratch_shapes=[
            pltpu.VMEM((pack.rows[0], LANES), F32),
            pltpu.VMEM((pack.rows[1], LANES), F32),
            pltpu.VMEM((3, width, width), BF16),
            pltpu.VMEM((k, width), F32),
            pltpu.VMEM((width, k), F32),
            pltpu.SemaphoreType.DMA((2, 2)),
        ],
        compiler_params=pltpu.CompilerParams(vmem_limit_bytes=28 * MIB),
        name="refine",
    )


def to_all(piece, axes):
    copies = jnp.broadcast_to(piece, (lax.axis_size(axes), *piece.shape))
    return lax.all_to_all(copies, axes, 0, 0, tiled=True)


def body(tokens, sketch_map, test_matrix):
    tokens_dev, width = tokens.shape
    k = sketch_map.shape[1]
    strip = width // lax.axis_size(("x", "z", "c"))
    total_tokens = tokens_dev * lax.axis_size(ALL)
    plane = lax.axis_size(("x", "y"))
    pack = Packing(width, 2 * plane)
    swap = [(0, 1), (1, 0)]
    held = [
        pltpu.with_memory_space_constraint(array, pltpu.HBM)
        for array in (tokens, sketch_map, test_matrix)
    ]
    tokens, pieces = held[0], []
    for stream in range(2):
        operands = (tokens, *held[1:]) if not stream else (tokens,)
        with jax.named_scope("products_%d" % stream):
            keep, send = local_products(pack, stream, width, tokens_dev, k)(*operands)
            if stream:
                send, arrived = lax.optimization_barrier((send, arrived))
                pieces.append(jnp.sum(arrived, axis=0))
        with jax.named_scope("over_core_%d" % stream):
            half = keep + lax.ppermute(send, "c", swap)
            if not stream:
                tokens, half = lax.optimization_barrier((tokens, half))
        with jax.named_scope("over_xy_%d" % stream):
            tiles = half.reshape(plane, pack.rows[stream] // 2 // plane, LANES)
            arrived = lax.all_to_all(tiles, ("x", "y"), 0, 0, tiled=True)
    pieces.append(jnp.sum(arrived, axis=0))
    with jax.named_scope("over_z"):
        piece = jnp.sum(to_all(jnp.concatenate(pieces, axis=0), "z"), axis=0)
    cut = pieces[0].shape[0]
    with jax.named_scope("back_0"):
        mine_0 = to_all(piece[:cut], ("x", "y"))
        mine_0, later = lax.optimization_barrier((mine_0, piece[cut:]))
        mine_0 = mine_0.reshape(-1, LANES)
    with jax.named_scope("back_1"):
        mine_1 = to_all(later, ("x", "y")).reshape(-1, LANES)
    with jax.named_scope("first_basis"):
        other_0 = lax.ppermute(mine_0, "c", swap)
        first = first_basis(pack, width, k)(mine_0, other_0)
    with jax.named_scope("refine"):
        mine_1, first = lax.optimization_barrier((mine_1, first))
        other_1 = lax.ppermute(mine_1, "c", swap)
        return refine(pack, width, k, strip, total_tokens)(
            mine_0, other_0, mine_1, other_1, first
        )


def solution(mesh):
    finer = Mesh(mesh.devices.reshape(4, 8, 2, mesh.shape["rep"]), ALL)
    return jax.shard_map(
        body,
        mesh=finer,
        in_specs=(P(ALL, None), P(ALL, None), P("y", None, None)),
        out_specs=(P(("x", "z", "c"), None), P()),
        check_vma=False,
    )
```

```python
import jax
import jax.numpy as jnp
from jax import lax
from jax.experimental import pallas as pl
from jax.experimental.pallas import tpu as pltpu
from jax.sharding import Mesh
from jax.sharding import PartitionSpec as P

ITERS = 2
ALL = ("x", "z", "c", "y")
LANES = 128
SUB = 8
PACKED = 16
MIB = 1024 * 1024
F32 = jnp.float32
BF16 = jnp.bfloat16
HI = lax.Precision.HIGHEST
NN = (((1,), (0,)), ((), ()))
NT = (((1,), (1,)), ((), ()))
TN = (((0,), (0,)), ((), ()))
ROUNDING = 2.0**-9
ALLOWED = 1.0e-3


class Packing:
    def __init__(self, width, pieces):
        self.n = width // LANES
        self.pieces = pieces
        count = self.n // 2
        self.pairs = list(range(count - 1, -1, -1))
        self.diagonal = self.n * LANES
        step = pieces * PACKED
        self.exact_rows = -(-(self.diagonal + self.n) // step) * step
        self.offset = {}
        at = 0
        for pair in self.pairs:
            left, right = 2 * pair, 2 * pair + 1
            for j in (left, right):
                for i in range(j):
                    self.offset[i, j] = at
                    at += LANES
            self.offset[left, left] = at
            at += LANES
        self.used = at
        self.cov_rows = -(-at // step) * step
        self.exact = self.exact_rows // pieces
        self.cov = self.cov_rows // pieces
        self.piece = 2 * self.exact + self.cov


def local_products(pack, width, tokens_dev, k):
    chunks = 4
    part = tokens_dev // chunks
    exact_half = pack.exact_rows // 2
    cov_half = pack.cov_rows // 2

    def kernel(
        tok_hbm, smap_hbm, test_hbm, keep_exact, keep_cov, send_exact, send_cov,
        tok, smap, test, exact, cov, rounded, sem, out_sem,
    ):
        core = lax.axis_index("c")
        slab = lax.axis_index(("x", "z", "c"))
        load_map = pltpu.make_async_copy(smap_hbm, smap, sem.at[chunks])
        load_test = pltpu.make_async_copy(
            test_hbm.at[0, pl.ds(pl.multiple_of(slab * k, k), k)], test, sem.at[chunks + 1]
        )
        loads = []
        for s in range(chunks):
            rows = pl.ds(s * part, part)
            loads.append(pltpu.make_async_copy(tok_hbm.at[rows], tok.at[rows], sem.at[s]))
        load_map.start()
        for load in loads:
            load.start()
        load_test.start()
        load_map.wait()
        sketch = jnp.zeros((k, width), F32)
        for s in range(chunks):
            loads[s].wait()
            rows = slice(s * part, (s + 1) * part)
            sketch = sketch + lax.dot_general(
                smap[rows, :], tok[rows, :], TN, preferred_element_type=F32
            )
        load_test.wait()
        start = lax.dot_general(test[...], sketch.astype(BF16), TN, preferred_element_type=F32)
        for i in range(pack.n):
            at = i * LANES
            exact[at : at + LANES, :] = start[:, at : at + LANES]
        exact[pack.diagonal :, :] = jnp.zeros((pack.exact_rows - pack.diagonal, LANES), F32)
        if pack.used < pack.cov_rows:
            cov[pack.used :, :] = jnp.zeros((pack.cov_rows - pack.used, LANES), F32)
        row = lax.broadcasted_iota(jnp.int32, (LANES, LANES), 0)
        col = lax.broadcasted_iota(jnp.int32, (LANES, LANES), 1)
        for pair in pack.pairs:
            base = 2 * pair * LANES
            high = base + 2 * LANES
            out = lax.dot_general(tok[:, :high], tok[:, base:high], TN, preferred_element_type=F32)
            for j in range(2):
                for i in range(2 * pair + j):
                    at = pack.offset[i, 2 * pair + j]
                    cov[at : at + LANES, :] = out[
                        i * LANES : (i + 1) * LANES, j * LANES : (j + 1) * LANES
                    ]
            upper = out[base : base + LANES, :LANES]
            lower = out[base + LANES : high, LANES:]
            at = pack.offset[2 * pair, 2 * pair]
            both = jnp.where(row < col, upper, lower)
            cov[at : at + LANES, :] = jnp.where(row == col, 0.0, both)
            for b, own in ((2 * pair, upper), (2 * pair + 1, lower)):
                line = jnp.sum(jnp.where(row == col, own, 0.0), axis=0)[None, :]
                exact[pack.diagonal + b : pack.diagonal + b + 1, :] = line
        away = 1 - core
        rounded[...] = cov[pl.ds(pl.multiple_of(away * cov_half, LANES), cov_half), :].astype(BF16)
        outs = []
        for from_ref, to in (
            (rounded, send_cov),
            (exact.at[pl.ds(pl.multiple_of(away * exact_half, LANES), exact_half)], send_exact),
            (exact.at[pl.ds(pl.multiple_of(core * exact_half, LANES), exact_half)], keep_exact),
            (cov.at[pl.ds(pl.multiple_of(core * cov_half, LANES), cov_half)], keep_cov),
        ):
            outs.append(pltpu.make_async_copy(from_ref, to, out_sem.at[len(outs)]))
        for copy in outs:
            copy.start()
        for copy in outs:
            copy.wait()

    return pl.pallas_call(
        kernel,
        out_shape=(
            jax.ShapeDtypeStruct((exact_half, LANES), F32),
            jax.ShapeDtypeStruct((cov_half, LANES), F32),
            jax.ShapeDtypeStruct((exact_half, LANES), F32),
            jax.ShapeDtypeStruct((cov_half, LANES), BF16),
        ),
        in_specs=[pl.BlockSpec(memory_space=pl.ANY)] * 3,
        out_specs=[pl.BlockSpec(memory_space=pl.ANY)] * 4,
        scratch_shapes=[
            pltpu.VMEM((tokens_dev, width), BF16),
            pltpu.VMEM((tokens_dev, k), BF16),
            pltpu.VMEM((k, k), BF16),
            pltpu.VMEM((pack.exact_rows, LANES), F32),
            pltpu.VMEM((pack.cov_rows, LANES), F32),
            pltpu.VMEM((cov_half, LANES), BF16),
            pltpu.SemaphoreType.DMA((chunks + 2,)),
            pltpu.SemaphoreType.DMA((4,)),
        ],
        compiler_params=pltpu.CompilerParams(vmem_limit_bytes=24 * MIB),
        name="local_products",
    )


def eliminate(gram):
    k = gram.shape[0]
    blocks = k // SUB
    lane = lax.broadcasted_iota(jnp.int32, (SUB, k), 1)
    row = lax.broadcasted_iota(jnp.int32, (SUB, k), 0)
    work, trace = [], []
    for b in range(blocks):
        work.append(gram[b * SUB : (b + 1) * SUB, :])
        trace.append(jnp.where(lane == row + b * SUB, 1.0, 0.0).astype(F32))
    factor, inverse = [], []
    for b in range(blocks):
        at = b * SUB
        spread = {}
        for o in range(b, blocks):
            for q in range(SUB):
                spread[o, q] = jnp.broadcast_to(work[o][:, at + q : at + q + 1], (SUB, k))
        d = {(p, q): spread[b, q][p : p + 1, :] for p in range(SUB) for q in range(p, SUB)}
        scale = []
        for p in range(SUB):
            scale.append(lax.rsqrt(d[p, p]))
            for q in range(p + 1, SUB):
                d[p, q] = d[p, q] * scale[p]
            for q in range(p + 1, SUB):
                for s in range(q, SUB):
                    d[q, s] = d[q, s] - d[p, q] * d[p, s]
        ra = [work[b][p : p + 1, :] for p in range(SUB)]
        re = [trace[b][p : p + 1, :] for p in range(SUB)]
        for p in range(SUB):
            ra[p] = ra[p] * scale[p]
            re[p] = re[p] * scale[p]
            for q in range(p + 1, SUB):
                ra[q] = ra[q] - d[p, q] * ra[p]
                re[q] = re[q] - d[p, q] * re[p]
        for o in range(b + 1, blocks):
            column = [spread[o, q] for q in range(SUB)]
            for p in range(SUB):
                column[p] = column[p] * scale[p]
                for q in range(p + 1, SUB):
                    column[q] = column[q] - d[p, q] * column[p]
                work[o] = work[o] - column[p] * ra[p]
                trace[o] = trace[o] - column[p] * re[p]
        factor.append(jnp.where(lane >= row + at, jnp.concatenate(ra, axis=0), 0.0))
        inverse.append(jnp.concatenate(re, axis=0))
    return jnp.concatenate(factor, axis=0), jnp.concatenate(inverse, axis=0)


def orthonormal(pt):
    gram = lax.dot_general(pt, pt, NT, precision=HI, preferred_element_type=F32)
    factor, inverse = eliminate(gram)
    return jnp.dot(inverse, pt, precision=HI, preferred_element_type=F32), factor, inverse


def packed_rows(ref, begin, count, length):
    found = []
    at = begin
    while at < begin + count:
        piece, row = at // length, at % length
        take = min(length - row, begin + count - at)
        found.append(ref[piece, row : row + take, :])
        at += take
    return found[0] if len(found) == 1 else jnp.concatenate(found, axis=0)


def refine(pack, width, k, strip, total_tokens):
    n = pack.n
    half = pack.pieces // 2

    def kernel(
        mine, other, basis, factor_out, first_out, error_out,
        value, rest, cov, dense, squares, zt, vt, turned, sem,
    ):
        core = lax.axis_index("c")
        slab = lax.axis_index(("x", "z", "c"))
        exact_at = pl.ds(0, pack.exact)
        rest_at = pl.ds(pack.exact, pack.exact)
        cov_at = pl.ds(2 * pack.exact, pack.cov)
        loads = []
        for side, home in ((mine, core), (other, 1 - core)):
            place = pl.ds(home * half, half)
            for rows, to in ((exact_at, value), (rest_at, rest), (cov_at, cov)):
                loads.append(
                    pltpu.make_async_copy(side.at[:, rows], to.at[place], sem.at[len(loads)])
                )
        for load in loads:
            load.start()
        for at in (0, 1, 3, 4):
            loads[at].wait()

        def exact_rows(begin, count):
            return packed_rows(value, begin, count, pack.exact).astype(F32) + packed_rows(
                rest, begin, count, pack.exact
            ).astype(F32)

        for i in range(n):
            zt[:, i * LANES : (i + 1) * LANES] = exact_rows(i * LANES, LANES)
        lines = exact_rows(pack.diagonal, PACKED)
        diagonal = jnp.concatenate([lines[i : i + 1, :] for i in range(n)], axis=1)

        def unpack():
            row = lax.broadcasted_iota(jnp.int32, (LANES, LANES), 0)
            col = lax.broadcasted_iota(jnp.int32, (LANES, LANES), 1)
            sums = [jnp.zeros((1, LANES), F32) for _ in range(n)]

            def put(i, j, v):
                dense[i * LANES : (i + 1) * LANES, j * LANES : (j + 1) * LANES] = v.astype(BF16)
                square = v * v
                sums[j] = sums[j] + jnp.sum(square, axis=0)[None, :]
                if i != j:
                    across = jnp.sum(square, axis=1, keepdims=True)
                    sums[i] = sums[i] + across.T

            for (i, j), at in pack.offset.items():
                v = packed_rows(cov, at, LANES, pack.cov).astype(F32)
                if i < j:
                    put(i, j, v)
                else:
                    flipped = v.T
                    put(i, i, jnp.where(row < col, v, flipped))
                    put(i + 1, i + 1, jnp.where(row > col, v, flipped))
            squares[...] = jnp.concatenate(sums, axis=1)

        error_out[...] = jnp.zeros(error_out.shape, F32)

        @pl.loop(0, ITERS + 1)
        def _(step):
            fresh, factor, inverse = orthonormal(zt[...])
            factor_out[...] = factor

            @pl.when(step == 0)
            def _():
                first_out[...] = fresh
                for at in (2, 5):
                    loads[at].wait()
                unpack()

            @pl.when(step > 0)
            def _():
                back = jnp.dot(inverse, vt[...], precision=HI, preferred_element_type=F32)
                share = (squares[...] * (1.0 / total_tokens) ** 2) * (back * back)
                line = jnp.sum(share, axis=0)[None, :]
                total = jnp.sum(line, axis=1, keepdims=True) * (ROUNDING**2 / k)
                error_out[...] = error_out[...] + jnp.broadcast_to(total, error_out.shape)

            vt[...] = fresh

            @pl.when(step < ITERS)
            def _():
                vb = fresh.astype(BF16)
                for j in range(n):
                    high = (j + 1) * LANES
                    rj = slice(j * LANES, high)
                    z = vb[:, rj].astype(F32) * diagonal[:, rj]
                    z = z + lax.dot_general(
                        vb[:, :high], dense[:high, rj], NN, preferred_element_type=F32
                    )
                    if j + 1 < n:
                        z = z + lax.dot_general(
                            vb[:, high:], dense[rj, high:], NT, preferred_element_type=F32
                        )
                    zt[:, rj] = z * (1.0 / total_tokens)

        for i in range(n):
            cols = slice(i * LANES, (i + 1) * LANES)
            turned[cols, :] = vt[:, cols].T
        basis[...] = turned[pl.ds(slab * strip, strip), :]

    return pl.pallas_call(
        kernel,
        out_shape=(
            jax.ShapeDtypeStruct((strip, k), F32),
            jax.ShapeDtypeStruct((k, k), F32),
            jax.ShapeDtypeStruct((k, width), F32),
            jax.ShapeDtypeStruct((SUB, LANES), F32),
        ),
        in_specs=[pl.BlockSpec(memory_space=pl.ANY)] * 2,
        out_specs=[pl.BlockSpec(memory_space=pltpu.VMEM)] * 4,
        scratch_shapes=[
            pltpu.VMEM((pack.pieces, pack.exact, LANES), BF16),
            pltpu.VMEM((pack.pieces, pack.exact, LANES), BF16),
            pltpu.VMEM((pack.pieces, pack.cov, LANES), BF16),
            pltpu.VMEM((width, width), BF16),
            pltpu.VMEM((1, width), F32),
            pltpu.VMEM((k, width), F32),
            pltpu.VMEM((k, width), F32),
            pltpu.VMEM((width, k), F32),
            pltpu.SemaphoreType.DMA((6,)),
        ],
        compiler_params=pltpu.CompilerParams(vmem_limit_bytes=28 * MIB),
        name="refine",
    )


def orthonormal_rows(zt):
    def kernel(zt_ref, vt_ref, factor_ref):
        vt, factor, _ = orthonormal(zt_ref[...])
        vt_ref[...] = vt
        factor_ref[...] = factor

    k = zt.shape[0]
    return pl.pallas_call(
        kernel,
        out_shape=(jax.ShapeDtypeStruct(zt.shape, F32), jax.ShapeDtypeStruct((k, k), F32)),
        compiler_params=pltpu.CompilerParams(vmem_limit_bytes=8 * MIB),
        name="orthonormal_rows",
    )(zt)


def direct(tokens, first, strip, total_tokens):
    k = first.shape[0]

    def step(_, state):
        vb = state[0].astype(BF16)
        projected = lax.dot_general(tokens, vb, NT, preferred_element_type=F32).astype(BF16)
        local = lax.dot_general(projected, tokens, TN, preferred_element_type=F32)
        return orthonormal_rows(lax.psum(local, ALL) / total_tokens)

    vt, factor = lax.fori_loop(0, ITERS, step, (first, jnp.zeros((k, k), F32)))
    slab = lax.axis_index(("x", "z", "c"))
    return lax.dynamic_slice_in_dim(vt, slab * strip, strip, 1).T, factor


def to_all(piece, axes):
    copies = jnp.broadcast_to(piece, (lax.axis_size(axes), *piece.shape))
    return lax.all_to_all(copies, axes, 0, 0, tiled=True)


def sendable(exact, cov, pieces):
    value = lax.reduce_precision(exact, exponent_bits=8, mantissa_bits=7)
    parts = [value, exact - value, cov]
    tiles = [part.astype(BF16).reshape(pieces, -1, LANES) for part in parts]
    return jnp.concatenate(tiles, axis=1)


def summed(arrived, pack):
    total = jnp.sum(arrived.astype(F32), axis=0)
    exact = total[: pack.exact] + total[pack.exact : 2 * pack.exact]
    return sendable(exact, total[2 * pack.exact :], 1)[0]


def body(tokens, sketch_map, test_matrix):
    tokens_dev, width = tokens.shape
    k = sketch_map.shape[1]
    strip = width // lax.axis_size(("x", "z", "c"))
    total_tokens = tokens_dev * lax.axis_size(ALL)
    plane = lax.axis_size(("x", "y"))
    pack = Packing(width, 2 * plane)
    swap = [(0, 1), (1, 0)]
    with jax.named_scope("products"):
        held = [
            pltpu.with_memory_space_constraint(array, pltpu.HBM)
            for array in (tokens, sketch_map, test_matrix)
        ]
        keep_exact, keep_cov, send_exact, send_cov = local_products(pack, width, tokens_dev, k)(
            *held
        )
    with jax.named_scope("over_core"):
        exact = keep_exact + lax.ppermute(send_exact, "c", swap)
        cov = keep_cov + lax.ppermute(send_cov, "c", swap).astype(F32)
        tiles = sendable(exact, cov, plane)
    with jax.named_scope("over_xy"):
        piece = summed(lax.all_to_all(tiles, ("x", "y"), 0, 0, tiled=True), pack)
    with jax.named_scope("over_z"):
        piece = summed(to_all(piece, "z"), pack)
    with jax.named_scope("back_xy"):
        mine = to_all(piece, ("x", "y"))
    with jax.named_scope("back_core"):
        other = lax.ppermute(mine, "c", swap)
    with jax.named_scope("refine"):
        basis, factor, first, error = refine(pack, width, k, strip, total_tokens)(mine, other)
    with jax.named_scope("check"):
        return lax.cond(
            error[0, 0] <= ALLOWED**2,
            lambda: (basis, factor),
            lambda: direct(tokens, first, strip, total_tokens),
        )


def solution(mesh):
    finer = Mesh(mesh.devices.reshape(4, 8, 2, mesh.shape["rep"]), ALL)
    return jax.shard_map(
        body,
        mesh=finer,
        in_specs=(P(ALL, None), P(ALL, None), P("y", None, None)),
        out_specs=(P(("x", "z", "c"), None), P()),
        check_vma=False,
    )
```

```python
import jax
import jax.numpy as jnp
from jax import lax
from jax.experimental import pallas as pl
from jax.experimental.pallas import tpu as pltpu
from jax.sharding import Mesh
from jax.sharding import PartitionSpec as P

ITERS = 2
ALL = ("x", "z", "c", "y")
LANES = 128
SUB = 8
PACKED = 16
MIB = 1024 * 1024
F32 = jnp.float32
BF16 = jnp.bfloat16
HI = lax.Precision.HIGHEST
NN = (((1,), (0,)), ((), ()))
NT = (((1,), (1,)), ((), ()))
TN = (((0,), (0,)), ((), ()))
ROUNDING = 2.0**-9
ALLOWED = 1.0e-3


class Packing:
    def __init__(self, width, pieces):
        self.n = width // LANES
        self.pieces = pieces
        count = self.n // 2
        self.pairs = list(range(count - 1, -1, -1))
        self.diagonal = self.n * LANES
        step = pieces * PACKED
        self.exact_rows = -(-(self.diagonal + self.n) // step) * step
        self.offset = {}
        at = 0
        for pair in self.pairs:
            left, right = 2 * pair, 2 * pair + 1
            for j in (left, right):
                for i in range(j):
                    self.offset[i, j] = at
                    at += LANES
            self.offset[left, left] = at
            at += LANES
        self.used = at
        self.cov_rows = -(-at // step) * step
        self.exact = self.exact_rows // pieces
        self.cov = self.cov_rows // pieces
        self.piece = 2 * self.exact + self.cov


def local_products(pack, width, tokens_dev, k):
    chunks = 4
    part = tokens_dev // chunks
    exact_half = pack.exact_rows // 2
    cov_half = pack.cov_rows // 2

    def kernel(
        tok_hbm, smap_hbm, test_hbm, keep_exact, keep_cov, send_exact, send_cov,
        tok, smap, test, exact, cov, rounded, sem, out_sem,
    ):
        core = lax.axis_index("c")
        slab = lax.axis_index(("x", "z", "c"))
        load_map = pltpu.make_async_copy(smap_hbm, smap, sem.at[chunks])
        load_test = pltpu.make_async_copy(
            test_hbm.at[0, pl.ds(pl.multiple_of(slab * k, k), k)], test, sem.at[chunks + 1]
        )
        loads = []
        for s in range(chunks):
            rows = pl.ds(s * part, part)
            loads.append(pltpu.make_async_copy(tok_hbm.at[rows], tok.at[rows], sem.at[s]))
        load_map.start()
        for load in loads:
            load.start()
        load_test.start()
        load_map.wait()
        sketch = jnp.zeros((k, width), F32)
        for s in range(chunks):
            loads[s].wait()
            rows = slice(s * part, (s + 1) * part)
            sketch = sketch + lax.dot_general(
                smap[rows, :], tok[rows, :], TN, preferred_element_type=F32
            )
        load_test.wait()
        start = lax.dot_general(test[...], sketch.astype(BF16), TN, preferred_element_type=F32)
        for i in range(pack.n):
            at = i * LANES
            exact[at : at + LANES, :] = start[:, at : at + LANES]
        exact[pack.diagonal :, :] = jnp.zeros((pack.exact_rows - pack.diagonal, LANES), F32)
        if pack.used < pack.cov_rows:
            cov[pack.used :, :] = jnp.zeros((pack.cov_rows - pack.used, LANES), F32)
        row = lax.broadcasted_iota(jnp.int32, (LANES, LANES), 0)
        col = lax.broadcasted_iota(jnp.int32, (LANES, LANES), 1)
        for pair in pack.pairs:
            base = 2 * pair * LANES
            high = base + 2 * LANES
            out = lax.dot_general(tok[:, :high], tok[:, base:high], TN, preferred_element_type=F32)
            for j in range(2):
                for i in range(2 * pair + j):
                    at = pack.offset[i, 2 * pair + j]
                    cov[at : at + LANES, :] = out[
                        i * LANES : (i + 1) * LANES, j * LANES : (j + 1) * LANES
                    ]
            upper = out[base : base + LANES, :LANES]
            lower = out[base + LANES : high, LANES:]
            at = pack.offset[2 * pair, 2 * pair]
            both = jnp.where(row < col, upper, lower)
            cov[at : at + LANES, :] = jnp.where(row == col, 0.0, both)
            for b, own in ((2 * pair, upper), (2 * pair + 1, lower)):
                line = jnp.sum(jnp.where(row == col, own, 0.0), axis=0)[None, :]
                exact[pack.diagonal + b : pack.diagonal + b + 1, :] = line
        away = 1 - core
        rounded[...] = cov[pl.ds(pl.multiple_of(away * cov_half, LANES), cov_half), :].astype(BF16)
        outs = []
        for from_ref, to in (
            (rounded, send_cov),
            (exact.at[pl.ds(pl.multiple_of(away * exact_half, LANES), exact_half)], send_exact),
            (exact.at[pl.ds(pl.multiple_of(core * exact_half, LANES), exact_half)], keep_exact),
            (cov.at[pl.ds(pl.multiple_of(core * cov_half, LANES), cov_half)], keep_cov),
        ):
            outs.append(pltpu.make_async_copy(from_ref, to, out_sem.at[len(outs)]))
        for copy in outs:
            copy.start()
        for copy in outs:
            copy.wait()

    return pl.pallas_call(
        kernel,
        out_shape=(
            jax.ShapeDtypeStruct((exact_half, LANES), F32),
            jax.ShapeDtypeStruct((cov_half, LANES), F32),
            jax.ShapeDtypeStruct((exact_half, LANES), F32),
            jax.ShapeDtypeStruct((cov_half, LANES), BF16),
        ),
        in_specs=[pl.BlockSpec(memory_space=pl.ANY)] * 3,
        out_specs=[pl.BlockSpec(memory_space=pl.ANY)] * 4,
        scratch_shapes=[
            pltpu.VMEM((tokens_dev, width), BF16),
            pltpu.VMEM((tokens_dev, k), BF16),
            pltpu.VMEM((k, k), BF16),
            pltpu.VMEM((pack.exact_rows, LANES), F32),
            pltpu.VMEM((pack.cov_rows, LANES), F32),
            pltpu.VMEM((cov_half, LANES), BF16),
            pltpu.SemaphoreType.DMA((chunks + 2,)),
            pltpu.SemaphoreType.DMA((4,)),
        ],
        compiler_params=pltpu.CompilerParams(vmem_limit_bytes=24 * MIB),
        name="local_products",
    )


def eliminate(gram):
    k = gram.shape[0]
    blocks = k // SUB
    lane = lax.broadcasted_iota(jnp.int32, (SUB, k), 1)
    row = lax.broadcasted_iota(jnp.int32, (SUB, k), 0)
    work, trace = [], []
    for b in range(blocks):
        work.append(gram[b * SUB : (b + 1) * SUB, :])
        trace.append(jnp.where(lane == row + b * SUB, 1.0, 0.0).astype(F32))
    factor, inverse = [], []
    for b in range(blocks):
        at = b * SUB
        spread = {}
        for o in range(b, blocks):
            for q in range(SUB):
                spread[o, q] = jnp.broadcast_to(work[o][:, at + q : at + q + 1], (SUB, k))
        d = {(p, q): spread[b, q][p : p + 1, :] for p in range(SUB) for q in range(p, SUB)}
        scale = []
        for p in range(SUB):
            scale.append(lax.rsqrt(d[p, p]))
            for q in range(p + 1, SUB):
                d[p, q] = d[p, q] * scale[p]
            for q in range(p + 1, SUB):
                for s in range(q, SUB):
                    d[q, s] = d[q, s] - d[p, q] * d[p, s]
        ra = [work[b][p : p + 1, :] for p in range(SUB)]
        re = [trace[b][p : p + 1, :] for p in range(SUB)]
        for p in range(SUB):
            ra[p] = ra[p] * scale[p]
            re[p] = re[p] * scale[p]
            for q in range(p + 1, SUB):
                ra[q] = ra[q] - d[p, q] * ra[p]
                re[q] = re[q] - d[p, q] * re[p]
        for o in range(b + 1, blocks):
            column = [spread[o, q] for q in range(SUB)]
            for p in range(SUB):
                column[p] = column[p] * scale[p]
                for q in range(p + 1, SUB):
                    column[q] = column[q] - d[p, q] * column[p]
                work[o] = work[o] - column[p] * ra[p]
                trace[o] = trace[o] - column[p] * re[p]
        factor.append(jnp.where(lane >= row + at, jnp.concatenate(ra, axis=0), 0.0))
        inverse.append(jnp.concatenate(re, axis=0))
    return jnp.concatenate(factor, axis=0), jnp.concatenate(inverse, axis=0)


def orthonormal(pt):
    gram = lax.dot_general(pt, pt, NT, precision=HI, preferred_element_type=F32)
    factor, inverse = eliminate(gram)
    return jnp.dot(inverse, pt, precision=HI, preferred_element_type=F32), factor, inverse


def packed_rows(ref, begin, count, length):
    found = []
    at = begin
    while at < begin + count:
        piece, row = at // length, at % length
        take = min(length - row, begin + count - at)
        found.append(ref[piece, row : row + take, :])
        at += take
    return found[0] if len(found) == 1 else jnp.concatenate(found, axis=0)


def refine(pack, width, k, strip, total_tokens):
    n = pack.n
    half = pack.pieces // 2

    def kernel(
        mine, other, basis, factor_out, first_out, error_out,
        value, rest, cov, dense, squares, zt, vt, turned, sem,
    ):
        core = lax.axis_index("c")
        slab = lax.axis_index(("x", "z", "c"))
        exact_at = pl.ds(0, pack.exact)
        rest_at = pl.ds(pack.exact, pack.exact)
        cov_at = pl.ds(2 * pack.exact, pack.cov)
        loads = []
        for side, home in ((mine, core), (other, 1 - core)):
            place = pl.ds(home * half, half)
            for rows, to in ((exact_at, value), (rest_at, rest), (cov_at, cov)):
                loads.append(
                    pltpu.make_async_copy(side.at[:, rows], to.at[place], sem.at[len(loads)])
                )
        for load in loads:
            load.start()
        for at in (0, 1, 3, 4):
            loads[at].wait()

        def exact_rows(begin, count):
            return packed_rows(value, begin, count, pack.exact).astype(F32) + packed_rows(
                rest, begin, count, pack.exact
            ).astype(F32)

        for i in range(n):
            zt[:, i * LANES : (i + 1) * LANES] = exact_rows(i * LANES, LANES)
        lines = exact_rows(pack.diagonal, PACKED)
        diagonal = jnp.concatenate([lines[i : i + 1, :] for i in range(n)], axis=1)

        def unpack():
            row = lax.broadcasted_iota(jnp.int32, (LANES, LANES), 0)
            col = lax.broadcasted_iota(jnp.int32, (LANES, LANES), 1)
            down = [jnp.zeros((1, LANES), F32) for _ in range(n)]
            across = [None] * n

            def put(i, j, v):
                dense[i * LANES : (i + 1) * LANES, j * LANES : (j + 1) * LANES] = v.astype(BF16)
                square = v * v
                down[j] = down[j] + jnp.sum(square, axis=0)[None, :]
                if i != j:
                    across[i] = square if across[i] is None else across[i] + square

            for (i, j), at in sorted(pack.offset.items()):
                v = packed_rows(cov, at, LANES, pack.cov).astype(F32)
                if i < j:
                    put(i, j, v)
                else:
                    flipped = v.T
                    put(i, i, jnp.where(row < col, v, flipped))
                    put(i + 1, i + 1, jnp.where(row > col, v, flipped))
            for i in range(n):
                if across[i] is not None:
                    down[i] = down[i] + jnp.sum(across[i].T, axis=0)[None, :]
            squares[...] = jnp.concatenate(down, axis=1)

        error_out[...] = jnp.zeros(error_out.shape, F32)

        @pl.loop(0, ITERS + 1)
        def _(step):
            fresh, factor, inverse = orthonormal(zt[...])
            factor_out[...] = factor

            @pl.when(step == 0)
            def _():
                first_out[...] = fresh
                for at in (2, 5):
                    loads[at].wait()
                unpack()

            @pl.when(step > 0)
            def _():
                back = jnp.dot(
                    inverse.astype(BF16), vt[...].astype(BF16), preferred_element_type=F32
                )
                share = (squares[...] * (1.0 / total_tokens) ** 2) * (back * back)
                line = jnp.sum(share, axis=0)[None, :]
                total = jnp.sum(line, axis=1, keepdims=True) * (ROUNDING**2 / k)
                error_out[...] = error_out[...] + jnp.broadcast_to(total, error_out.shape)

            vt[...] = fresh

            @pl.when(step < ITERS)
            def _():
                vb = fresh.astype(BF16)
                for j in range(n):
                    high = (j + 1) * LANES
                    rj = slice(j * LANES, high)
                    z = vb[:, rj].astype(F32) * diagonal[:, rj]
                    z = z + lax.dot_general(
                        vb[:, :high], dense[:high, rj], NN, preferred_element_type=F32
                    )
                    if j + 1 < n:
                        z = z + lax.dot_general(
                            vb[:, high:], dense[rj, high:], NT, preferred_element_type=F32
                        )
                    zt[:, rj] = z * (1.0 / total_tokens)

        for i in range(n):
            cols = slice(i * LANES, (i + 1) * LANES)
            turned[cols, :] = vt[:, cols].T
        basis[...] = turned[pl.ds(slab * strip, strip), :]

    return pl.pallas_call(
        kernel,
        out_shape=(
            jax.ShapeDtypeStruct((strip, k), F32),
            jax.ShapeDtypeStruct((k, k), F32),
            jax.ShapeDtypeStruct((k, width), F32),
            jax.ShapeDtypeStruct((SUB, LANES), F32),
        ),
        in_specs=[pl.BlockSpec(memory_space=pl.ANY)] * 2,
        out_specs=[pl.BlockSpec(memory_space=pltpu.VMEM)] * 4,
        scratch_shapes=[
            pltpu.VMEM((pack.pieces, pack.exact, LANES), BF16),
            pltpu.VMEM((pack.pieces, pack.exact, LANES), BF16),
            pltpu.VMEM((pack.pieces, pack.cov, LANES), BF16),
            pltpu.VMEM((width, width), BF16),
            pltpu.VMEM((1, width), F32),
            pltpu.VMEM((k, width), F32),
            pltpu.VMEM((k, width), F32),
            pltpu.VMEM((width, k), F32),
            pltpu.SemaphoreType.DMA((6,)),
        ],
        compiler_params=pltpu.CompilerParams(vmem_limit_bytes=28 * MIB),
        name="refine",
    )


def orthonormal_rows(zt):
    def kernel(zt_ref, vt_ref, factor_ref):
        vt, factor, _ = orthonormal(zt_ref[...])
        vt_ref[...] = vt
        factor_ref[...] = factor

    k = zt.shape[0]
    return pl.pallas_call(
        kernel,
        out_shape=(jax.ShapeDtypeStruct(zt.shape, F32), jax.ShapeDtypeStruct((k, k), F32)),
        compiler_params=pltpu.CompilerParams(vmem_limit_bytes=8 * MIB),
        name="orthonormal_rows",
    )(zt)


def direct(tokens, first, strip, total_tokens):
    k = first.shape[0]

    def step(_, state):
        vb = state[0].astype(BF16)
        projected = lax.dot_general(tokens, vb, NT, preferred_element_type=F32).astype(BF16)
        local = lax.dot_general(projected, tokens, TN, preferred_element_type=F32)
        tiles = local.reshape(lax.axis_size(ALL), -1, LANES)
        share = jnp.sum(lax.all_to_all(tiles, ALL, 0, 0, tiled=True), axis=0)
        return orthonormal_rows(to_all(share, ALL).reshape(local.shape) / total_tokens)

    vt, factor = lax.fori_loop(0, ITERS, step, (first, jnp.zeros((k, k), F32)))
    slab = lax.axis_index(("x", "z", "c"))
    return lax.dynamic_slice_in_dim(vt, slab * strip, strip, 1).T, factor


def to_all(piece, axes):
    copies = jnp.broadcast_to(piece, (lax.axis_size(axes), *piece.shape))
    return lax.all_to_all(copies, axes, 0, 0, tiled=True)


def sendable(exact, cov, pieces):
    value = lax.reduce_precision(exact, exponent_bits=8, mantissa_bits=7)
    parts = [value, exact - value, cov]
    tiles = [part.astype(BF16).reshape(pieces, -1, LANES) for part in parts]
    return jnp.concatenate(tiles, axis=1)


def summed(arrived, pack):
    total = jnp.sum(arrived.astype(F32), axis=0)
    exact = total[: pack.exact] + total[pack.exact : 2 * pack.exact]
    return sendable(exact, total[2 * pack.exact :], 1)[0]


def body(tokens, sketch_map, test_matrix):
    tokens_dev, width = tokens.shape
    k = sketch_map.shape[1]
    strip = width // lax.axis_size(("x", "z", "c"))
    total_tokens = tokens_dev * lax.axis_size(ALL)
    plane = lax.axis_size(("x", "y"))
    pack = Packing(width, 2 * plane)
    swap = [(0, 1), (1, 0)]
    with jax.named_scope("products"):
        held = [
            pltpu.with_memory_space_constraint(array, pltpu.HBM)
            for array in (tokens, sketch_map, test_matrix)
        ]
        keep_exact, keep_cov, send_exact, send_cov = local_products(pack, width, tokens_dev, k)(
            *held
        )
    with jax.named_scope("over_core"):
        exact = keep_exact + lax.ppermute(send_exact, "c", swap)
        cov = keep_cov + lax.ppermute(send_cov, "c", swap).astype(F32)
        tiles = sendable(exact, cov, plane)
    with jax.named_scope("over_xy"):
        piece = summed(lax.all_to_all(tiles, ("x", "y"), 0, 0, tiled=True), pack)
    with jax.named_scope("over_z"):
        piece = summed(to_all(piece, "z"), pack)
    with jax.named_scope("back_xy"):
        mine = to_all(piece, ("x", "y"))
    with jax.named_scope("back_core"):
        other = lax.ppermute(mine, "c", swap)
    with jax.named_scope("refine"):
        basis, factor, first, error = refine(pack, width, k, strip, total_tokens)(mine, other)
    with jax.named_scope("check"):
        return lax.cond(
            error[0, 0] <= ALLOWED**2,
            lambda: (basis, factor),
            lambda: direct(tokens, first, strip, total_tokens),
        )


def solution(mesh):
    finer = Mesh(mesh.devices.reshape(4, 8, 2, mesh.shape["rep"]), ALL)
    return jax.shard_map(
        body,
        mesh=finer,
        in_specs=(P(ALL, None), P(ALL, None), P("y", None, None)),
        out_specs=(P(("x", "z", "c"), None), P()),
        check_vma=False,
    )
```

```python
import jax
import jax.numpy as jnp
from jax import lax
from jax.experimental import pallas as pl
from jax.experimental.pallas import tpu as pltpu
from jax.sharding import Mesh
from jax.sharding import PartitionSpec as P

ITERS = 2
ALL = ("x", "z", "c", "y")
LANES = 128
SUB = 8
PACKED = 16
MIB = 1024 * 1024
F32 = jnp.float32
BF16 = jnp.bfloat16
HI = lax.Precision.HIGHEST
NN = (((1,), (0,)), ((), ()))
NT = (((1,), (1,)), ((), ()))
TN = (((0,), (0,)), ((), ()))
ROUNDING = 2.0**-9
ALLOWED = 1.0e-3


class Packing:
    def __init__(self, width, pieces):
        self.n = width // LANES
        self.pieces = pieces
        count = self.n // 2
        self.pairs = list(range(count - 1, -1, -1))
        self.diagonal = self.n * LANES
        step = pieces * PACKED
        self.exact_rows = -(-(self.diagonal + self.n) // step) * step
        self.offset = {}
        at = 0
        for pair in self.pairs:
            left, right = 2 * pair, 2 * pair + 1
            for j in (left, right):
                for i in range(j):
                    self.offset[i, j] = at
                    at += LANES
            self.offset[left, left] = at
            at += LANES
        self.used = at
        self.cov_rows = -(-at // step) * step
        self.exact = self.exact_rows // pieces
        self.cov = self.cov_rows // pieces
        self.piece = 2 * self.exact + self.cov


def local_products(pack, width, tokens_dev, k):
    chunks = 4
    part = tokens_dev // chunks
    exact_half = pack.exact_rows // 2
    cov_half = pack.cov_rows // 2

    def kernel(
        tok_hbm, smap_hbm, test_hbm, keep_exact, keep_cov, send_exact, send_cov,
        tok, smap, test, exact, cov, rounded, sem, out_sem,
    ):
        core = lax.axis_index("c")
        slab = lax.axis_index(("x", "z", "c"))
        load_map = pltpu.make_async_copy(smap_hbm, smap, sem.at[chunks])
        load_test = pltpu.make_async_copy(
            test_hbm.at[0, pl.ds(pl.multiple_of(slab * k, k), k)], test, sem.at[chunks + 1]
        )
        loads = []
        for s in range(chunks):
            rows = pl.ds(s * part, part)
            loads.append(pltpu.make_async_copy(tok_hbm.at[rows], tok.at[rows], sem.at[s]))
        load_map.start()
        for load in loads:
            load.start()
        load_test.start()
        load_map.wait()
        sketch = jnp.zeros((k, width), F32)
        for s in range(chunks):
            loads[s].wait()
            rows = slice(s * part, (s + 1) * part)
            sketch = sketch + lax.dot_general(
                smap[rows, :], tok[rows, :], TN, preferred_element_type=F32
            )
        load_test.wait()
        start = lax.dot_general(test[...], sketch.astype(BF16), TN, preferred_element_type=F32)
        for i in range(pack.n):
            at = i * LANES
            exact[at : at + LANES, :] = start[:, at : at + LANES]
        exact[pack.diagonal :, :] = jnp.zeros((pack.exact_rows - pack.diagonal, LANES), F32)
        if pack.used < pack.cov_rows:
            cov[pack.used :, :] = jnp.zeros((pack.cov_rows - pack.used, LANES), F32)
        row = lax.broadcasted_iota(jnp.int32, (LANES, LANES), 0)
        col = lax.broadcasted_iota(jnp.int32, (LANES, LANES), 1)
        for pair in pack.pairs:
            base = 2 * pair * LANES
            high = base + 2 * LANES
            out = lax.dot_general(tok[:, :high], tok[:, base:high], TN, preferred_element_type=F32)
            for j in range(2):
                for i in range(2 * pair + j):
                    at = pack.offset[i, 2 * pair + j]
                    cov[at : at + LANES, :] = out[
                        i * LANES : (i + 1) * LANES, j * LANES : (j + 1) * LANES
                    ]
            upper = out[base : base + LANES, :LANES]
            lower = out[base + LANES : high, LANES:]
            at = pack.offset[2 * pair, 2 * pair]
            both = jnp.where(row < col, upper, lower)
            cov[at : at + LANES, :] = jnp.where(row == col, 0.0, both)
            for b, own in ((2 * pair, upper), (2 * pair + 1, lower)):
                line = jnp.sum(jnp.where(row == col, own, 0.0), axis=0)[None, :]
                exact[pack.diagonal + b : pack.diagonal + b + 1, :] = line
        away = 1 - core
        rounded[...] = cov[pl.ds(pl.multiple_of(away * cov_half, LANES), cov_half), :].astype(BF16)
        outs = []
        for from_ref, to in (
            (rounded, send_cov),
            (exact.at[pl.ds(pl.multiple_of(away * exact_half, LANES), exact_half)], send_exact),
            (exact.at[pl.ds(pl.multiple_of(core * exact_half, LANES), exact_half)], keep_exact),
            (cov.at[pl.ds(pl.multiple_of(core * cov_half, LANES), cov_half)], keep_cov),
        ):
            outs.append(pltpu.make_async_copy(from_ref, to, out_sem.at[len(outs)]))
        for copy in outs:
            copy.start()
        for copy in outs:
            copy.wait()

    return pl.pallas_call(
        kernel,
        out_shape=(
            jax.ShapeDtypeStruct((exact_half, LANES), F32),
            jax.ShapeDtypeStruct((cov_half, LANES), F32),
            jax.ShapeDtypeStruct((exact_half, LANES), F32),
            jax.ShapeDtypeStruct((cov_half, LANES), BF16),
        ),
        in_specs=[pl.BlockSpec(memory_space=pl.ANY)] * 3,
        out_specs=[pl.BlockSpec(memory_space=pl.ANY)] * 4,
        scratch_shapes=[
            pltpu.VMEM((tokens_dev, width), BF16),
            pltpu.VMEM((tokens_dev, k), BF16),
            pltpu.VMEM((k, k), BF16),
            pltpu.VMEM((pack.exact_rows, LANES), F32),
            pltpu.VMEM((pack.cov_rows, LANES), F32),
            pltpu.VMEM((cov_half, LANES), BF16),
            pltpu.SemaphoreType.DMA((chunks + 2,)),
            pltpu.SemaphoreType.DMA((4,)),
        ],
        compiler_params=pltpu.CompilerParams(vmem_limit_bytes=24 * MIB),
        name="local_products",
    )


def eliminate(gram):
    k = gram.shape[0]
    blocks = k // SUB
    segment = blocks // 2
    lane = lax.broadcasted_iota(jnp.int32, (SUB, k), 1)
    row = lax.broadcasted_iota(jnp.int32, (SUB, k), 0)
    work, trace = [], []
    for b in range(blocks):
        work.append(gram[b * SUB : (b + 1) * SUB, :])
        trace.append(jnp.where(lane == row + b * SUB, 1.0, 0.0).astype(F32))
    factor, inverse = [], []
    for b in range(blocks):
        at = b * SUB
        stop = (b // segment + 1) * segment
        spread = {}
        for o in range(b, stop):
            for q in range(SUB):
                spread[o, q] = jnp.broadcast_to(work[o][:, at + q : at + q + 1], (SUB, k))
        d = {(p, q): spread[b, q][p : p + 1, :] for p in range(SUB) for q in range(p, SUB)}
        scale = []
        for p in range(SUB):
            scale.append(lax.rsqrt(d[p, p]))
            for q in range(p + 1, SUB):
                d[p, q] = d[p, q] * scale[p]
            for q in range(p + 1, SUB):
                for s in range(q, SUB):
                    d[q, s] = d[q, s] - d[p, q] * d[p, s]
        ra = [work[b][p : p + 1, :] for p in range(SUB)]
        re = [trace[b][p : p + 1, :] for p in range(SUB)]
        for p in range(SUB):
            ra[p] = ra[p] * scale[p]
            re[p] = re[p] * scale[p]
            for q in range(p + 1, SUB):
                ra[q] = ra[q] - d[p, q] * ra[p]
                re[q] = re[q] - d[p, q] * re[p]
        for o in range(b + 1, stop):
            column = [spread[o, q] for q in range(SUB)]
            for p in range(SUB):
                column[p] = column[p] * scale[p]
                for q in range(p + 1, SUB):
                    column[q] = column[q] - d[p, q] * column[p]
                work[o] = work[o] - column[p] * ra[p]
                trace[o] = trace[o] - column[p] * re[p]
        factor.append(jnp.concatenate(ra, axis=0))
        inverse.append(jnp.concatenate(re, axis=0))
        if b + 1 == stop and stop < blocks:
            above = jnp.concatenate(factor[-segment:], axis=0)
            beside = jnp.concatenate([above, jnp.concatenate(inverse[-segment:], axis=0)], axis=1)
            update = lax.dot_general(above, beside, TN, precision=HI, preferred_element_type=F32)
            for o in range(stop, blocks):
                rows = slice(o * SUB, (o + 1) * SUB)
                work[o] = work[o] - update[rows, :k]
                trace[o] = trace[o] - update[rows, k:]
    for b in range(blocks):
        factor[b] = jnp.where(lane >= row + b * SUB, factor[b], 0.0)
    return jnp.concatenate(factor, axis=0), jnp.concatenate(inverse, axis=0)


def orthonormal(pt):
    gram = lax.dot_general(pt, pt, NT, precision=HI, preferred_element_type=F32)
    factor, inverse = eliminate(gram)
    return jnp.dot(inverse, pt, precision=HI, preferred_element_type=F32), factor, inverse


def packed_rows(ref, begin, count, length):
    found = []
    at = begin
    while at < begin + count:
        piece, row = at // length, at % length
        take = min(length - row, begin + count - at)
        found.append(ref[piece, row : row + take, :])
        at += take
    return found[0] if len(found) == 1 else jnp.concatenate(found, axis=0)


def refine(pack, width, k, strip, total_tokens):
    n = pack.n
    half = pack.pieces // 2

    def kernel(
        mine, other, basis, factor_out, first_out, fine_out,
        value, rest, cov, dense, squares, error, zt, vt, turned, sem,
    ):
        core = lax.axis_index("c")
        slab = lax.axis_index(("x", "z", "c"))
        exact_at = pl.ds(0, pack.exact)
        rest_at = pl.ds(pack.exact, pack.exact)
        cov_at = pl.ds(2 * pack.exact, pack.cov)
        loads = []
        for side, home in ((mine, core), (other, 1 - core)):
            place = pl.ds(home * half, half)
            for rows, to in ((exact_at, value), (rest_at, rest), (cov_at, cov)):
                loads.append(
                    pltpu.make_async_copy(side.at[:, rows], to.at[place], sem.at[len(loads)])
                )
        for load in loads:
            load.start()
        for at in (0, 1, 3, 4):
            loads[at].wait()

        def exact_rows(begin, count):
            return packed_rows(value, begin, count, pack.exact).astype(F32) + packed_rows(
                rest, begin, count, pack.exact
            ).astype(F32)

        for i in range(n):
            zt[:, i * LANES : (i + 1) * LANES] = exact_rows(i * LANES, LANES)
        lines = exact_rows(pack.diagonal, PACKED)
        diagonal = jnp.concatenate([lines[i : i + 1, :] for i in range(n)], axis=1)

        def unpack():
            row = lax.broadcasted_iota(jnp.int32, (LANES, LANES), 0)
            col = lax.broadcasted_iota(jnp.int32, (LANES, LANES), 1)
            down = [jnp.zeros((1, LANES), F32) for _ in range(n)]
            across = [None] * n

            def put(i, j, v):
                dense[i * LANES : (i + 1) * LANES, j * LANES : (j + 1) * LANES] = v.astype(BF16)
                square = v * v
                down[j] = down[j] + jnp.sum(square, axis=0)[None, :]
                if i != j:
                    across[i] = square if across[i] is None else across[i] + square

            for (i, j), at in sorted(pack.offset.items()):
                v = packed_rows(cov, at, LANES, pack.cov).astype(F32)
                if i < j:
                    put(i, j, v)
                else:
                    flipped = v.T
                    put(i, i, jnp.where(row < col, v, flipped))
                    put(i + 1, i + 1, jnp.where(row > col, v, flipped))
            for i in range(n):
                if across[i] is not None:
                    down[i] = down[i] + jnp.sum(across[i].T, axis=0)[None, :]
            squares[...] = jnp.concatenate(down, axis=1)

        error[...] = jnp.zeros(error.shape, F32)

        @pl.loop(0, ITERS + 1)
        def _(step):
            fresh, factor, inverse = orthonormal(zt[...])
            factor_out[...] = factor

            @pl.when(step == 0)
            def _():
                first_out[...] = fresh
                for at in (2, 5):
                    loads[at].wait()
                unpack()

            @pl.when(step > 0)
            def _():
                back = jnp.dot(
                    inverse.astype(BF16), vt[...].astype(BF16), preferred_element_type=F32
                )
                share = (squares[...] * (1.0 / total_tokens) ** 2) * (back * back)
                line = jnp.sum(share, axis=0)[None, :]
                total = jnp.sum(line, axis=1, keepdims=True) * (ROUNDING**2 / k)
                error[...] = error[...] + jnp.broadcast_to(total, error.shape)

            vt[...] = fresh

            @pl.when(step < ITERS)
            def _():
                vb = fresh.astype(BF16)
                for j in range(n):
                    high = (j + 1) * LANES
                    rj = slice(j * LANES, high)
                    z = vb[:, rj].astype(F32) * diagonal[:, rj]
                    z = z + lax.dot_general(
                        vb[:, :high], dense[:high, rj], NN, preferred_element_type=F32
                    )
                    if j + 1 < n:
                        z = z + lax.dot_general(
                            vb[:, high:], dense[rj, high:], NT, preferred_element_type=F32
                        )
                    zt[:, rj] = z * (1.0 / total_tokens)

        for i in range(n):
            cols = slice(i * LANES, (i + 1) * LANES)
            turned[cols, :] = vt[:, cols].T
        basis[...] = turned[pl.ds(slab * strip, strip), :]
        fine_out[0] = (jnp.sum(error[:1, :1]) <= ALLOWED**2).astype(jnp.int32)

    return pl.pallas_call(
        kernel,
        out_shape=(
            jax.ShapeDtypeStruct((strip, k), F32),
            jax.ShapeDtypeStruct((k, k), F32),
            jax.ShapeDtypeStruct((k, width), F32),
            jax.ShapeDtypeStruct((1,), jnp.int32),
        ),
        in_specs=[pl.BlockSpec(memory_space=pl.ANY)] * 2,
        out_specs=[pl.BlockSpec(memory_space=pltpu.VMEM)] * 3
        + [pl.BlockSpec(memory_space=pltpu.SMEM)],
        scratch_shapes=[
            pltpu.VMEM((pack.pieces, pack.exact, LANES), BF16),
            pltpu.VMEM((pack.pieces, pack.exact, LANES), BF16),
            pltpu.VMEM((pack.pieces, pack.cov, LANES), BF16),
            pltpu.VMEM((width, width), BF16),
            pltpu.VMEM((1, width), F32),
            pltpu.VMEM((SUB, LANES), F32),
            pltpu.VMEM((k, width), F32),
            pltpu.VMEM((k, width), F32),
            pltpu.VMEM((width, k), F32),
            pltpu.SemaphoreType.DMA((6,)),
        ],
        compiler_params=pltpu.CompilerParams(vmem_limit_bytes=28 * MIB),
        name="refine",
    )


def orthonormal_rows(zt):
    def kernel(zt_ref, vt_ref, factor_ref):
        vt, factor, _ = orthonormal(zt_ref[...])
        vt_ref[...] = vt
        factor_ref[...] = factor

    k = zt.shape[0]
    return pl.pallas_call(
        kernel,
        out_shape=(jax.ShapeDtypeStruct(zt.shape, F32), jax.ShapeDtypeStruct((k, k), F32)),
        compiler_params=pltpu.CompilerParams(vmem_limit_bytes=8 * MIB),
        name="orthonormal_rows",
    )(zt)


def direct(tokens, first, strip, total_tokens):
    k = first.shape[0]

    def step(_, state):
        vb = state[0].astype(BF16)
        projected = lax.dot_general(tokens, vb, NT, preferred_element_type=F32).astype(BF16)
        local = lax.dot_general(projected, tokens, TN, preferred_element_type=F32)
        tiles = local.reshape(lax.axis_size(ALL), -1, LANES)
        share = jnp.sum(lax.all_to_all(tiles, ALL, 0, 0, tiled=True), axis=0)
        return orthonormal_rows(to_all(share, ALL).reshape(local.shape) / total_tokens)

    vt, factor = lax.fori_loop(0, ITERS, step, (first, jnp.zeros((k, k), F32)))
    slab = lax.axis_index(("x", "z", "c"))
    return lax.dynamic_slice_in_dim(vt, slab * strip, strip, 1).T, factor


def to_all(piece, axes):
    copies = jnp.broadcast_to(piece, (lax.axis_size(axes), *piece.shape))
    return lax.all_to_all(copies, axes, 0, 0, tiled=True)


def sendable(exact, cov, pieces):
    value = lax.reduce_precision(exact, exponent_bits=8, mantissa_bits=7)
    parts = [value, exact - value, cov]
    tiles = [part.astype(BF16).reshape(pieces, -1, LANES) for part in parts]
    return jnp.concatenate(tiles, axis=1)


def summed(arrived, pack):
    total = jnp.sum(arrived.astype(F32), axis=0)
    exact = total[: pack.exact] + total[pack.exact : 2 * pack.exact]
    return sendable(exact, total[2 * pack.exact :], 1)[0]


def body(tokens, sketch_map, test_matrix):
    tokens_dev, width = tokens.shape
    k = sketch_map.shape[1]
    strip = width // lax.axis_size(("x", "z", "c"))
    total_tokens = tokens_dev * lax.axis_size(ALL)
    plane = lax.axis_size(("x", "y"))
    pack = Packing(width, 2 * plane)
    swap = [(0, 1), (1, 0)]
    with jax.named_scope("products"):
        held = [
            pltpu.with_memory_space_constraint(array, pltpu.HBM)
            for array in (tokens, sketch_map, test_matrix)
        ]
        keep_exact, keep_cov, send_exact, send_cov = local_products(pack, width, tokens_dev, k)(
            *held
        )
    with jax.named_scope("over_core"):
        exact = keep_exact + lax.ppermute(send_exact, "c", swap)
        cov = keep_cov + lax.ppermute(send_cov, "c", swap).astype(F32)
        tiles = sendable(exact, cov, plane)
    with jax.named_scope("over_xy"):
        piece = summed(lax.all_to_all(tiles, ("x", "y"), 0, 0, tiled=True), pack)
    with jax.named_scope("over_z"):
        piece = summed(to_all(piece, "z"), pack)
    with jax.named_scope("back_xy"):
        mine = to_all(piece, ("x", "y"))
    with jax.named_scope("back_core"):
        other = lax.ppermute(mine, "c", swap)
    with jax.named_scope("refine"):
        basis, factor, first, fine = refine(pack, width, k, strip, total_tokens)(mine, other)
    with jax.named_scope("check"):
        return lax.cond(
            fine[0] > 0,
            lambda: (basis, factor),
            lambda: direct(tokens, first, strip, total_tokens),
        )


def solution(mesh):
    finer = Mesh(mesh.devices.reshape(4, 8, 2, mesh.shape["rep"]), ALL)
    return jax.shard_map(
        body,
        mesh=finer,
        in_specs=(P(ALL, None), P(ALL, None), P("y", None, None)),
        out_specs=(P(("x", "z", "c"), None), P()),
        check_vma=False,
    )
```

```python
import jax
import jax.numpy as jnp
from jax import lax
from jax.experimental import pallas as pl
from jax.experimental.pallas import tpu as pltpu
from jax.sharding import Mesh
from jax.sharding import PartitionSpec as P

ITERS = 2
ALL = ("x", "z", "c", "y")
LANES = 128
SUB = 8
PACKED = 16
MIB = 1024 * 1024
F32 = jnp.float32
BF16 = jnp.bfloat16
HI = lax.Precision.HIGHEST
NN = (((1,), (0,)), ((), ()))
NT = (((1,), (1,)), ((), ()))
TN = (((0,), (0,)), ((), ()))
ROUNDING = 2.0**-9
ALLOWED = 1.0e-3


class Packing:
    def __init__(self, width, pieces):
        self.n = width // LANES
        self.pieces = pieces
        count = self.n // 2
        self.pairs = list(range(count - 1, -1, -1))
        self.diagonal = self.n * LANES
        step = pieces * PACKED
        self.exact_rows = -(-(self.diagonal + self.n) // step) * step
        self.offset = {}
        at = 0
        for pair in self.pairs:
            left, right = 2 * pair, 2 * pair + 1
            for j in (left, right):
                for i in range(j):
                    self.offset[i, j] = at
                    at += LANES
            self.offset[left, left] = at
            at += LANES
        self.used = at
        self.cov_rows = -(-at // step) * step
        self.exact = self.exact_rows // pieces
        self.cov = self.cov_rows // pieces
        self.piece = 2 * self.exact + self.cov


def local_products(pack, width, tokens_dev, k):
    chunks = 4
    part = tokens_dev // chunks
    exact_half = pack.exact_rows // 2
    cov_half = pack.cov_rows // 2

    def kernel(
        tok_hbm, smap_hbm, test_hbm, keep_exact, keep_cov, send_exact, send_cov,
        tok, smap, test, exact, cov, own, rounded, sem, out_sem,
    ):
        core = lax.axis_index("c")
        slab = lax.axis_index(("x", "z", "c"))
        load_map = pltpu.make_async_copy(smap_hbm, smap, sem.at[chunks])
        load_test = pltpu.make_async_copy(
            test_hbm.at[0, pl.ds(pl.multiple_of(slab * k, k), k)], test, sem.at[chunks + 1]
        )
        loads = []
        for s in range(chunks):
            rows = pl.ds(s * part, part)
            loads.append(pltpu.make_async_copy(tok_hbm.at[rows], tok.at[rows], sem.at[s]))
        load_map.start()
        for load in loads:
            load.start()
        load_test.start()
        load_map.wait()
        sketch = jnp.zeros((k, width), F32)
        for s in range(chunks):
            loads[s].wait()
            rows = slice(s * part, (s + 1) * part)
            sketch = sketch + lax.dot_general(
                smap[rows, :], tok[rows, :], TN, preferred_element_type=F32
            )
            if (s + 1) % (chunks // 2) == 0:
                rows = slice((s + 1 - chunks // 2) * part, (s + 1) * part)
                opening = s < chunks // 2
                for pair in pack.pairs:
                    base = 2 * pair * LANES
                    high = base + 2 * LANES
                    out = lax.dot_general(
                        tok[rows, :high], tok[rows, base:high], TN, preferred_element_type=F32
                    )
                    for j in range(2):
                        col = 2 * pair + j
                        for i in range(col + 1):
                            tile = out[i * LANES : (i + 1) * LANES, j * LANES : (j + 1) * LANES]
                            to = own if i == col else cov
                            at = col * LANES if i == col else pack.offset[i, col]
                            place = slice(at, at + LANES)
                            to[place, :] = tile if opening else to[place, :] + tile
        load_test.wait()
        start = lax.dot_general(test[...], sketch.astype(BF16), TN, preferred_element_type=F32)
        for i in range(pack.n):
            at = i * LANES
            exact[at : at + LANES, :] = start[:, at : at + LANES]
        exact[pack.diagonal :, :] = jnp.zeros((pack.exact_rows - pack.diagonal, LANES), F32)
        if pack.used < pack.cov_rows:
            cov[pack.used :, :] = jnp.zeros((pack.cov_rows - pack.used, LANES), F32)
        row = lax.broadcasted_iota(jnp.int32, (LANES, LANES), 0)
        col = lax.broadcasted_iota(jnp.int32, (LANES, LANES), 1)
        for pair in pack.pairs:
            base = 2 * pair * LANES
            upper = own[base : base + LANES, :]
            lower = own[base + LANES : base + 2 * LANES, :]
            at = pack.offset[2 * pair, 2 * pair]
            both = jnp.where(row < col, upper, lower)
            cov[at : at + LANES, :] = jnp.where(row == col, 0.0, both)
            for b, block in ((2 * pair, upper), (2 * pair + 1, lower)):
                line = jnp.sum(jnp.where(row == col, block, 0.0), axis=0)[None, :]
                exact[pack.diagonal + b : pack.diagonal + b + 1, :] = line
        away = 1 - core
        rounded[...] = cov[pl.ds(pl.multiple_of(away * cov_half, LANES), cov_half), :].astype(BF16)
        outs = []
        for from_ref, to in (
            (rounded, send_cov),
            (exact.at[pl.ds(pl.multiple_of(away * exact_half, LANES), exact_half)], send_exact),
            (exact.at[pl.ds(pl.multiple_of(core * exact_half, LANES), exact_half)], keep_exact),
            (cov.at[pl.ds(pl.multiple_of(core * cov_half, LANES), cov_half)], keep_cov),
        ):
            outs.append(pltpu.make_async_copy(from_ref, to, out_sem.at[len(outs)]))
        for copy in outs:
            copy.start()
        for copy in outs:
            copy.wait()

    return pl.pallas_call(
        kernel,
        out_shape=(
            jax.ShapeDtypeStruct((exact_half, LANES), F32),
            jax.ShapeDtypeStruct((cov_half, LANES), F32),
            jax.ShapeDtypeStruct((exact_half, LANES), F32),
            jax.ShapeDtypeStruct((cov_half, LANES), BF16),
        ),
        in_specs=[pl.BlockSpec(memory_space=pl.ANY)] * 3,
        out_specs=[pl.BlockSpec(memory_space=pl.ANY)] * 4,
        scratch_shapes=[
            pltpu.VMEM((tokens_dev, width), BF16),
            pltpu.VMEM((tokens_dev, k), BF16),
            pltpu.VMEM((k, k), BF16),
            pltpu.VMEM((pack.exact_rows, LANES), F32),
            pltpu.VMEM((pack.cov_rows, LANES), F32),
            pltpu.VMEM((width, LANES), F32),
            pltpu.VMEM((cov_half, LANES), BF16),
            pltpu.SemaphoreType.DMA((chunks + 2,)),
            pltpu.SemaphoreType.DMA((4,)),
        ],
        compiler_params=pltpu.CompilerParams(vmem_limit_bytes=24 * MIB),
        name="local_products",
    )


def eliminate(gram):
    k = gram.shape[0]
    blocks = k // SUB
    segment = blocks // 2
    lane = lax.broadcasted_iota(jnp.int32, (SUB, k), 1)
    row = lax.broadcasted_iota(jnp.int32, (SUB, k), 0)
    work, trace = [], []
    for b in range(blocks):
        work.append(gram[b * SUB : (b + 1) * SUB, :])
        trace.append(jnp.where(lane == row + b * SUB, 1.0, 0.0).astype(F32))
    factor, inverse = [], []
    for b in range(blocks):
        at = b * SUB
        stop = (b // segment + 1) * segment
        spread = {}
        for o in range(b, stop):
            for q in range(SUB):
                spread[o, q] = jnp.broadcast_to(work[o][:, at + q : at + q + 1], (SUB, k))
        d = {(p, q): spread[b, q][p : p + 1, :] for p in range(SUB) for q in range(p, SUB)}
        scale = []
        for p in range(SUB):
            scale.append(lax.rsqrt(d[p, p]))
            for q in range(p + 1, SUB):
                d[p, q] = d[p, q] * scale[p]
            for q in range(p + 1, SUB):
                for s in range(q, SUB):
                    d[q, s] = d[q, s] - d[p, q] * d[p, s]
        ra = [work[b][p : p + 1, :] for p in range(SUB)]
        re = [trace[b][p : p + 1, :] for p in range(SUB)]
        for p in range(SUB):
            ra[p] = ra[p] * scale[p]
            re[p] = re[p] * scale[p]
            for q in range(p + 1, SUB):
                ra[q] = ra[q] - d[p, q] * ra[p]
                re[q] = re[q] - d[p, q] * re[p]
        for o in range(b + 1, stop):
            column = [spread[o, q] for q in range(SUB)]
            for p in range(SUB):
                column[p] = column[p] * scale[p]
                for q in range(p + 1, SUB):
                    column[q] = column[q] - d[p, q] * column[p]
                work[o] = work[o] - column[p] * ra[p]
                trace[o] = trace[o] - column[p] * re[p]
        factor.append(jnp.concatenate(ra, axis=0))
        inverse.append(jnp.concatenate(re, axis=0))
        if b + 1 == stop and stop < blocks:
            above = jnp.concatenate(factor[-segment:], axis=0)
            beside = jnp.concatenate([above, jnp.concatenate(inverse[-segment:], axis=0)], axis=1)
            update = lax.dot_general(above, beside, TN, precision=HI, preferred_element_type=F32)
            for o in range(stop, blocks):
                rows = slice(o * SUB, (o + 1) * SUB)
                work[o] = work[o] - update[rows, :k]
                trace[o] = trace[o] - update[rows, k:]
    for b in range(blocks):
        factor[b] = jnp.where(lane >= row + b * SUB, factor[b], 0.0)
    return jnp.concatenate(factor, axis=0), jnp.concatenate(inverse, axis=0)


def orthonormal(pt):
    gram = lax.dot_general(pt, pt, NT, precision=HI, preferred_element_type=F32)
    factor, inverse = eliminate(gram)
    return jnp.dot(inverse, pt, precision=HI, preferred_element_type=F32), factor, inverse


def packed_rows(ref, begin, count, length):
    found = []
    at = begin
    while at < begin + count:
        piece, row = at // length, at % length
        take = min(length - row, begin + count - at)
        found.append(ref[piece, row : row + take, :])
        at += take
    return found[0] if len(found) == 1 else jnp.concatenate(found, axis=0)


def refine(pack, width, k, strip, total_tokens):
    n = pack.n
    half = pack.pieces // 2

    def kernel(
        mine, other, basis, factor_out, first_out, fine_out,
        value, rest, cov, dense, squares, error, zt, vt, turned, sem,
    ):
        core = lax.axis_index("c")
        slab = lax.axis_index(("x", "z", "c"))
        exact_at = pl.ds(0, pack.exact)
        rest_at = pl.ds(pack.exact, pack.exact)
        cov_at = pl.ds(2 * pack.exact, pack.cov)
        loads = []
        for side, home in ((mine, core), (other, 1 - core)):
            place = pl.ds(home * half, half)
            for rows, to in ((exact_at, value), (rest_at, rest), (cov_at, cov)):
                loads.append(
                    pltpu.make_async_copy(side.at[:, rows], to.at[place], sem.at[len(loads)])
                )
        for load in loads:
            load.start()
        for at in (0, 1, 3, 4):
            loads[at].wait()

        def exact_rows(begin, count):
            return packed_rows(value, begin, count, pack.exact).astype(F32) + packed_rows(
                rest, begin, count, pack.exact
            ).astype(F32)

        for i in range(n):
            zt[:, i * LANES : (i + 1) * LANES] = exact_rows(i * LANES, LANES)
        lines = exact_rows(pack.diagonal, PACKED)
        diagonal = jnp.concatenate([lines[i : i + 1, :] for i in range(n)], axis=1)

        def unpack():
            row = lax.broadcasted_iota(jnp.int32, (LANES, LANES), 0)
            col = lax.broadcasted_iota(jnp.int32, (LANES, LANES), 1)
            down = [jnp.zeros((1, LANES), F32) for _ in range(n)]
            across = [None] * n

            def put(i, j, v):
                dense[i * LANES : (i + 1) * LANES, j * LANES : (j + 1) * LANES] = v.astype(BF16)
                square = v * v
                down[j] = down[j] + jnp.sum(square, axis=0)[None, :]
                if i != j:
                    across[i] = square if across[i] is None else across[i] + square

            for (i, j), at in sorted(pack.offset.items()):
                v = packed_rows(cov, at, LANES, pack.cov).astype(F32)
                if i < j:
                    put(i, j, v)
                else:
                    flipped = v.T
                    put(i, i, jnp.where(row < col, v, flipped))
                    put(i + 1, i + 1, jnp.where(row > col, v, flipped))
            for i in range(n):
                if across[i] is not None:
                    down[i] = down[i] + jnp.sum(across[i].T, axis=0)[None, :]
            squares[...] = jnp.concatenate(down, axis=1)

        error[...] = jnp.zeros(error.shape, F32)

        @pl.loop(0, ITERS + 1)
        def _(step):
            fresh, factor, inverse = orthonormal(zt[...])
            factor_out[...] = factor

            @pl.when(step == 0)
            def _():
                first_out[...] = fresh
                for at in (2, 5):
                    loads[at].wait()
                unpack()

            @pl.when(step > 0)
            def _():
                back = jnp.dot(
                    inverse.astype(BF16), vt[...].astype(BF16), preferred_element_type=F32
                )
                share = (squares[...] * (1.0 / total_tokens) ** 2) * (back * back)
                line = jnp.sum(share, axis=0)[None, :]
                total = jnp.sum(line, axis=1, keepdims=True) * (ROUNDING**2 / k)
                error[...] = error[...] + jnp.broadcast_to(total, error.shape)

            vt[...] = fresh

            @pl.when(step < ITERS)
            def _():
                vb = fresh.astype(BF16)
                for j in range(n):
                    high = (j + 1) * LANES
                    rj = slice(j * LANES, high)
                    z = vb[:, rj].astype(F32) * diagonal[:, rj]
                    z = z + lax.dot_general(
                        vb[:, :high], dense[:high, rj], NN, preferred_element_type=F32
                    )
                    if j + 1 < n:
                        z = z + lax.dot_general(
                            vb[:, high:], dense[rj, high:], NT, preferred_element_type=F32
                        )
                    zt[:, rj] = z * (1.0 / total_tokens)

        for i in range(n):
            cols = slice(i * LANES, (i + 1) * LANES)
            turned[cols, :] = vt[:, cols].T
        basis[...] = turned[pl.ds(slab * strip, strip), :]
        fine_out[0] = (jnp.sum(error[:1, :1]) <= ALLOWED**2).astype(jnp.int32)

    return pl.pallas_call(
        kernel,
        out_shape=(
            jax.ShapeDtypeStruct((strip, k), F32),
            jax.ShapeDtypeStruct((k, k), F32),
            jax.ShapeDtypeStruct((k, width), F32),
            jax.ShapeDtypeStruct((1,), jnp.int32),
        ),
        in_specs=[pl.BlockSpec(memory_space=pl.ANY)] * 2,
        out_specs=[pl.BlockSpec(memory_space=pltpu.VMEM)] * 3
        + [pl.BlockSpec(memory_space=pltpu.SMEM)],
        scratch_shapes=[
            pltpu.VMEM((pack.pieces, pack.exact, LANES), BF16),
            pltpu.VMEM((pack.pieces, pack.exact, LANES), BF16),
            pltpu.VMEM((pack.pieces, pack.cov, LANES), BF16),
            pltpu.VMEM((width, width), BF16),
            pltpu.VMEM((1, width), F32),
            pltpu.VMEM((SUB, LANES), F32),
            pltpu.VMEM((k, width), F32),
            pltpu.VMEM((k, width), F32),
            pltpu.VMEM((width, k), F32),
            pltpu.SemaphoreType.DMA((6,)),
        ],
        compiler_params=pltpu.CompilerParams(vmem_limit_bytes=28 * MIB),
        name="refine",
    )


def orthonormal_rows(zt):
    def kernel(zt_ref, vt_ref, factor_ref):
        vt, factor, _ = orthonormal(zt_ref[...])
        vt_ref[...] = vt
        factor_ref[...] = factor

    k = zt.shape[0]
    return pl.pallas_call(
        kernel,
        out_shape=(jax.ShapeDtypeStruct(zt.shape, F32), jax.ShapeDtypeStruct((k, k), F32)),
        compiler_params=pltpu.CompilerParams(vmem_limit_bytes=8 * MIB),
        name="orthonormal_rows",
    )(zt)


def direct(tokens, first, strip, total_tokens):
    k = first.shape[0]

    def step(_, state):
        vb = state[0].astype(BF16)
        projected = lax.dot_general(tokens, vb, NT, preferred_element_type=F32).astype(BF16)
        local = lax.dot_general(projected, tokens, TN, preferred_element_type=F32)
        tiles = local.reshape(lax.axis_size(ALL), -1, LANES)
        share = jnp.sum(lax.all_to_all(tiles, ALL, 0, 0, tiled=True), axis=0)
        return orthonormal_rows(to_all(share, ALL).reshape(local.shape) / total_tokens)

    vt, factor = lax.fori_loop(0, ITERS, step, (first, jnp.zeros((k, k), F32)))
    slab = lax.axis_index(("x", "z", "c"))
    return lax.dynamic_slice_in_dim(vt, slab * strip, strip, 1).T, factor


def to_all(piece, axes):
    copies = jnp.broadcast_to(piece, (lax.axis_size(axes), *piece.shape))
    return lax.all_to_all(copies, axes, 0, 0, tiled=True)


def sendable(exact, cov, pieces):
    value = lax.reduce_precision(exact, exponent_bits=8, mantissa_bits=7)
    parts = [value, exact - value, cov]
    tiles = [part.astype(BF16).reshape(pieces, -1, LANES) for part in parts]
    return jnp.concatenate(tiles, axis=1)


def summed(arrived, pack):
    total = jnp.sum(arrived.astype(F32), axis=0)
    exact = total[: pack.exact] + total[pack.exact : 2 * pack.exact]
    return sendable(exact, total[2 * pack.exact :], 1)[0]


def body(tokens, sketch_map, test_matrix):
    tokens_dev, width = tokens.shape
    k = sketch_map.shape[1]
    strip = width // lax.axis_size(("x", "z", "c"))
    total_tokens = tokens_dev * lax.axis_size(ALL)
    plane = lax.axis_size(("x", "y"))
    pack = Packing(width, 2 * plane)
    swap = [(0, 1), (1, 0)]
    with jax.named_scope("products"):
        held = [
            pltpu.with_memory_space_constraint(array, pltpu.HBM)
            for array in (tokens, sketch_map, test_matrix)
        ]
        keep_exact, keep_cov, send_exact, send_cov = local_products(pack, width, tokens_dev, k)(
            *held
        )
    with jax.named_scope("over_core"):
        exact = keep_exact + lax.ppermute(send_exact, "c", swap)
        cov = keep_cov + lax.ppermute(send_cov, "c", swap).astype(F32)
        tiles = sendable(exact, cov, plane)
    with jax.named_scope("over_xy"):
        piece = summed(lax.all_to_all(tiles, ("x", "y"), 0, 0, tiled=True), pack)
    with jax.named_scope("over_z"):
        piece = summed(to_all(piece, "z"), pack)
    with jax.named_scope("back_xy"):
        mine = to_all(piece, ("x", "y"))
    with jax.named_scope("back_core"):
        other = lax.ppermute(mine, "c", swap)
    with jax.named_scope("refine"):
        basis, factor, first, fine = refine(pack, width, k, strip, total_tokens)(mine, other)
    with jax.named_scope("check"):
        return lax.cond(
            fine[0] > 0,
            lambda: (basis, factor),
            lambda: direct(tokens, first, strip, total_tokens),
        )


def solution(mesh):
    finer = Mesh(mesh.devices.reshape(4, 8, 2, mesh.shape["rep"]), ALL)
    return jax.shard_map(
        body,
        mesh=finer,
        in_specs=(P(ALL, None), P(ALL, None), P("y", None, None)),
        out_specs=(P(("x", "z", "c"), None), P()),
        check_vma=False,
    )
```

```python
import jax
import jax.numpy as jnp
from jax import lax
from jax.experimental import pallas as pl
from jax.experimental.pallas import tpu as pltpu
from jax.sharding import Mesh
from jax.sharding import PartitionSpec as P

ITERS = 2
ALL = ("x", "z", "c", "y")
LANES = 128
SUB = 8
PACKED = 16
MIB = 1024 * 1024
F32 = jnp.float32
BF16 = jnp.bfloat16
HI = lax.Precision.HIGHEST
NN = (((1,), (0,)), ((), ()))
NT = (((1,), (1,)), ((), ()))
TN = (((0,), (0,)), ((), ()))
ROUNDING = 2.0**-9
ALLOWED = 1.0e-3


class Packing:
    def __init__(self, width, pieces):
        self.n = width // LANES
        self.pieces = pieces
        count = self.n // 2
        self.pairs = list(range(count - 1, -1, -1))
        self.diagonal = self.n * LANES
        step = pieces * PACKED
        self.exact_rows = -(-(self.diagonal + self.n) // step) * step
        self.offset = {}
        at = 0
        for pair in self.pairs:
            left, right = 2 * pair, 2 * pair + 1
            for j in (left, right):
                for i in range(j):
                    self.offset[i, j] = at
                    at += LANES
            self.offset[left, left] = at
            at += LANES
        self.used = at
        self.cov_rows = -(-at // step) * step
        self.exact = self.exact_rows // pieces
        self.cov = self.cov_rows // pieces
        self.piece = 2 * self.exact + self.cov


def local_products(pack, width, tokens_dev, k):
    chunks = 4
    part = tokens_dev // chunks
    exact_half = pack.exact_rows // 2
    cov_half = pack.cov_rows // 2

    def kernel(
        tok_hbm, smap_hbm, test_hbm, keep_exact, keep_cov, send_exact, send_cov,
        tok, smap, test, exact, cov, rounded, sem, out_sem,
    ):
        core = lax.axis_index("c")
        slab = lax.axis_index(("x", "z", "c"))
        load_map = pltpu.make_async_copy(smap_hbm, smap, sem.at[chunks])
        load_test = pltpu.make_async_copy(
            test_hbm.at[0, pl.ds(pl.multiple_of(slab * k, k), k)], test, sem.at[chunks + 1]
        )
        loads = []
        for s in range(chunks):
            rows = pl.ds(s * part, part)
            loads.append(pltpu.make_async_copy(tok_hbm.at[rows], tok.at[rows], sem.at[s]))
        load_map.start()
        for load in loads:
            load.start()
        load_test.start()
        load_map.wait()
        sketch = jnp.zeros((k, width), F32)
        for s in range(chunks):
            loads[s].wait()
            rows = slice(s * part, (s + 1) * part)
            sketch = sketch + lax.dot_general(
                smap[rows, :], tok[rows, :], TN, preferred_element_type=F32
            )
        load_test.wait()
        start = lax.dot_general(test[...], sketch.astype(BF16), TN, preferred_element_type=F32)
        for i in range(pack.n):
            at = i * LANES
            exact[at : at + LANES, :] = start[:, at : at + LANES]
        exact[pack.diagonal :, :] = jnp.zeros((pack.exact_rows - pack.diagonal, LANES), F32)
        if pack.used < pack.cov_rows:
            cov[pack.used :, :] = jnp.zeros((pack.cov_rows - pack.used, LANES), F32)
        row = lax.broadcasted_iota(jnp.int32, (LANES, LANES), 0)
        col = lax.broadcasted_iota(jnp.int32, (LANES, LANES), 1)
        for pair in pack.pairs:
            base = 2 * pair * LANES
            high = base + 2 * LANES
            out = lax.dot_general(tok[:, :high], tok[:, base:high], TN, preferred_element_type=F32)
            for j in range(2):
                for i in range(2 * pair + j):
                    at = pack.offset[i, 2 * pair + j]
                    cov[at : at + LANES, :] = out[
                        i * LANES : (i + 1) * LANES, j * LANES : (j + 1) * LANES
                    ]
            upper = out[base : base + LANES, :LANES]
            lower = out[base + LANES : high, LANES:]
            at = pack.offset[2 * pair, 2 * pair]
            both = jnp.where(row < col, upper, lower)
            cov[at : at + LANES, :] = jnp.where(row == col, 0.0, both)
            for b, own in ((2 * pair, upper), (2 * pair + 1, lower)):
                line = jnp.sum(jnp.where(row == col, own, 0.0), axis=0)[None, :]
                exact[pack.diagonal + b : pack.diagonal + b + 1, :] = line
        away = 1 - core
        rounded[...] = cov[pl.ds(pl.multiple_of(away * cov_half, LANES), cov_half), :].astype(BF16)
        outs = []
        for from_ref, to in (
            (rounded, send_cov),
            (exact.at[pl.ds(pl.multiple_of(away * exact_half, LANES), exact_half)], send_exact),
            (exact.at[pl.ds(pl.multiple_of(core * exact_half, LANES), exact_half)], keep_exact),
            (cov.at[pl.ds(pl.multiple_of(core * cov_half, LANES), cov_half)], keep_cov),
        ):
            outs.append(pltpu.make_async_copy(from_ref, to, out_sem.at[len(outs)]))
        for copy in outs:
            copy.start()
        for copy in outs:
            copy.wait()

    return pl.pallas_call(
        kernel,
        out_shape=(
            jax.ShapeDtypeStruct((exact_half, LANES), F32),
            jax.ShapeDtypeStruct((cov_half, LANES), F32),
            jax.ShapeDtypeStruct((exact_half, LANES), F32),
            jax.ShapeDtypeStruct((cov_half, LANES), BF16),
        ),
        in_specs=[pl.BlockSpec(memory_space=pl.ANY)] * 3,
        out_specs=[pl.BlockSpec(memory_space=pl.ANY)] * 4,
        scratch_shapes=[
            pltpu.VMEM((tokens_dev, width), BF16),
            pltpu.VMEM((tokens_dev, k), BF16),
            pltpu.VMEM((k, k), BF16),
            pltpu.VMEM((pack.exact_rows, LANES), F32),
            pltpu.VMEM((pack.cov_rows, LANES), F32),
            pltpu.VMEM((cov_half, LANES), BF16),
            pltpu.SemaphoreType.DMA((chunks + 2,)),
            pltpu.SemaphoreType.DMA((4,)),
        ],
        compiler_params=pltpu.CompilerParams(vmem_limit_bytes=24 * MIB),
        name="local_products",
    )


def eliminate(gram):
    k = gram.shape[0]
    blocks = k // SUB
    segment = blocks // 2
    lane = lax.broadcasted_iota(jnp.int32, (SUB, k), 1)
    row = lax.broadcasted_iota(jnp.int32, (SUB, k), 0)
    work, trace = [], []
    for b in range(blocks):
        work.append(gram[b * SUB : (b + 1) * SUB, :])
        trace.append(jnp.where(lane == row + b * SUB, 1.0, 0.0).astype(F32))
    factor, inverse = [], []
    for b in range(blocks):
        at = b * SUB
        stop = (b // segment + 1) * segment
        spread = {}
        for o in range(b, stop):
            for q in range(SUB):
                spread[o, q] = jnp.broadcast_to(work[o][:, at + q : at + q + 1], (SUB, k))
        d = {(p, q): spread[b, q][p : p + 1, :] for p in range(SUB) for q in range(p, SUB)}
        scale = []
        for p in range(SUB):
            scale.append(lax.rsqrt(d[p, p]))
            for q in range(p + 1, SUB):
                d[p, q] = d[p, q] * scale[p]
            for q in range(p + 1, SUB):
                for s in range(q, SUB):
                    d[q, s] = d[q, s] - d[p, q] * d[p, s]
        ra = [work[b][p : p + 1, :] for p in range(SUB)]
        re = [trace[b][p : p + 1, :] for p in range(SUB)]
        for p in range(SUB):
            ra[p] = ra[p] * scale[p]
            re[p] = re[p] * scale[p]
            for q in range(p + 1, SUB):
                ra[q] = ra[q] - d[p, q] * ra[p]
                re[q] = re[q] - d[p, q] * re[p]
        for o in range(b + 1, stop):
            column = [spread[o, q] for q in range(SUB)]
            for p in range(SUB):
                column[p] = column[p] * scale[p]
                for q in range(p + 1, SUB):
                    column[q] = column[q] - d[p, q] * column[p]
                work[o] = work[o] - column[p] * ra[p]
                trace[o] = trace[o] - column[p] * re[p]
        factor.append(jnp.concatenate(ra, axis=0))
        inverse.append(jnp.concatenate(re, axis=0))
        if b + 1 == stop and stop < blocks:
            above = jnp.concatenate(factor[-segment:], axis=0)
            beside = jnp.concatenate([above, jnp.concatenate(inverse[-segment:], axis=0)], axis=1)
            update = lax.dot_general(above, beside, TN, precision=HI, preferred_element_type=F32)
            for o in range(stop, blocks):
                rows = slice(o * SUB, (o + 1) * SUB)
                work[o] = work[o] - update[rows, :k]
                trace[o] = trace[o] - update[rows, k:]
    for b in range(blocks):
        factor[b] = jnp.where(lane >= row + b * SUB, factor[b], 0.0)
    return jnp.concatenate(factor, axis=0), jnp.concatenate(inverse, axis=0)


def thirds(v):
    high = v.astype(BF16)
    rest = v - high.astype(F32)
    mid = rest.astype(BF16)
    return high, mid, (rest - mid.astype(F32)).astype(BF16)


def orthonormal(pt):
    k = pt.shape[0]
    high, mid, low = thirds(pt)
    three = jnp.concatenate([high, mid, low], axis=0)
    wide = lax.dot_general(high, three, NT, preferred_element_type=F32)
    middle = lax.dot_general(mid, mid, NT, preferred_element_type=F32)
    cross = wide[:, 2 * k :] + wide[:, k : 2 * k]
    gram = wide[:, :k] + (cross + cross.T + middle)
    factor, inverse = eliminate(gram)
    ih, im, il = thirds(inverse)
    top = jnp.concatenate([high, mid], axis=0)
    ends = jnp.concatenate([low, high], axis=0)
    vt = jnp.dot(jnp.concatenate([ih, il], axis=1), ends, preferred_element_type=F32)
    vt = vt + jnp.dot(jnp.concatenate([im, im], axis=1), top, preferred_element_type=F32)
    vt = vt + jnp.dot(jnp.concatenate([ih, ih], axis=1), top, preferred_element_type=F32)
    return vt, factor, inverse


def packed_rows(ref, begin, count, length):
    found = []
    at = begin
    while at < begin + count:
        piece, row = at // length, at % length
        take = min(length - row, begin + count - at)
        found.append(ref[piece, row : row + take, :])
        at += take
    return found[0] if len(found) == 1 else jnp.concatenate(found, axis=0)


def refine(pack, width, k, strip, total_tokens):
    n = pack.n
    half = pack.pieces // 2

    def kernel(
        mine, other, basis, factor_out, first_out, fine_out,
        value, rest, cov, dense, squares, error, zt, vt, turned, sem,
    ):
        core = lax.axis_index("c")
        slab = lax.axis_index(("x", "z", "c"))
        exact_at = pl.ds(0, pack.exact)
        rest_at = pl.ds(pack.exact, pack.exact)
        cov_at = pl.ds(2 * pack.exact, pack.cov)
        loads = []
        for side, home in ((mine, core), (other, 1 - core)):
            place = pl.ds(home * half, half)
            for rows, to in ((exact_at, value), (rest_at, rest), (cov_at, cov)):
                loads.append(
                    pltpu.make_async_copy(side.at[:, rows], to.at[place], sem.at[len(loads)])
                )
        for load in loads:
            load.start()
        for at in (0, 1, 3, 4):
            loads[at].wait()

        def exact_rows(begin, count):
            return packed_rows(value, begin, count, pack.exact).astype(F32) + packed_rows(
                rest, begin, count, pack.exact
            ).astype(F32)

        for i in range(n):
            zt[:, i * LANES : (i + 1) * LANES] = exact_rows(i * LANES, LANES)
        lines = exact_rows(pack.diagonal, PACKED)
        diagonal = jnp.concatenate([lines[i : i + 1, :] for i in range(n)], axis=1)

        def unpack():
            row = lax.broadcasted_iota(jnp.int32, (LANES, LANES), 0)
            col = lax.broadcasted_iota(jnp.int32, (LANES, LANES), 1)
            down = [jnp.zeros((1, LANES), F32) for _ in range(n)]
            across = [None] * n

            def put(i, j, v):
                dense[i * LANES : (i + 1) * LANES, j * LANES : (j + 1) * LANES] = v.astype(BF16)
                square = v * v
                down[j] = down[j] + jnp.sum(square, axis=0)[None, :]
                if i != j:
                    across[i] = square if across[i] is None else across[i] + square

            for (i, j), at in sorted(pack.offset.items()):
                v = packed_rows(cov, at, LANES, pack.cov).astype(F32)
                if i < j:
                    put(i, j, v)
                else:
                    flipped = v.T
                    put(i, i, jnp.where(row < col, v, flipped))
                    put(i + 1, i + 1, jnp.where(row > col, v, flipped))
            for i in range(n):
                if across[i] is not None:
                    down[i] = down[i] + jnp.sum(across[i].T, axis=0)[None, :]
            squares[...] = jnp.concatenate(down, axis=1)

        error[...] = jnp.zeros(error.shape, F32)

        @pl.loop(0, ITERS + 1)
        def _(step):
            fresh, factor, inverse = orthonormal(zt[...])
            factor_out[...] = factor

            @pl.when(step == 0)
            def _():
                first_out[...] = fresh
                for at in (2, 5):
                    loads[at].wait()
                unpack()

            @pl.when(step > 0)
            def _():
                back = jnp.dot(
                    inverse.astype(BF16), vt[...].astype(BF16), preferred_element_type=F32
                )
                share = (squares[...] * (1.0 / total_tokens) ** 2) * (back * back)
                line = jnp.sum(share, axis=0)[None, :]
                total = jnp.sum(line, axis=1, keepdims=True) * (ROUNDING**2 / k)
                error[...] = error[...] + jnp.broadcast_to(total, error.shape)

            vt[...] = fresh

            @pl.when(step < ITERS)
            def _():
                vb = fresh.astype(BF16)
                for j in range(n):
                    high = (j + 1) * LANES
                    rj = slice(j * LANES, high)
                    z = vb[:, rj].astype(F32) * diagonal[:, rj]
                    z = z + lax.dot_general(
                        vb[:, :high], dense[:high, rj], NN, preferred_element_type=F32
                    )
                    if j + 1 < n:
                        z = z + lax.dot_general(
                            vb[:, high:], dense[rj, high:], NT, preferred_element_type=F32
                        )
                    zt[:, rj] = z * (1.0 / total_tokens)

        for i in range(n):
            cols = slice(i * LANES, (i + 1) * LANES)
            turned[cols, :] = vt[:, cols].T
        basis[...] = turned[pl.ds(slab * strip, strip), :]
        fine_out[0] = (jnp.sum(error[:1, :1]) <= ALLOWED**2).astype(jnp.int32)

    return pl.pallas_call(
        kernel,
        out_shape=(
            jax.ShapeDtypeStruct((strip, k), F32),
            jax.ShapeDtypeStruct((k, k), F32),
            jax.ShapeDtypeStruct((k, width), F32),
            jax.ShapeDtypeStruct((1,), jnp.int32),
        ),
        in_specs=[pl.BlockSpec(memory_space=pl.ANY)] * 2,
        out_specs=[pl.BlockSpec(memory_space=pltpu.VMEM)] * 3
        + [pl.BlockSpec(memory_space=pltpu.SMEM)],
        scratch_shapes=[
            pltpu.VMEM((pack.pieces, pack.exact, LANES), BF16),
            pltpu.VMEM((pack.pieces, pack.exact, LANES), BF16),
            pltpu.VMEM((pack.pieces, pack.cov, LANES), BF16),
            pltpu.VMEM((width, width), BF16),
            pltpu.VMEM((1, width), F32),
            pltpu.VMEM((SUB, LANES), F32),
            pltpu.VMEM((k, width), F32),
            pltpu.VMEM((k, width), F32),
            pltpu.VMEM((width, k), F32),
            pltpu.SemaphoreType.DMA((6,)),
        ],
        compiler_params=pltpu.CompilerParams(vmem_limit_bytes=28 * MIB),
        name="refine",
    )


def orthonormal_rows(zt):
    def kernel(zt_ref, vt_ref, factor_ref):
        vt, factor, _ = orthonormal(zt_ref[...])
        vt_ref[...] = vt
        factor_ref[...] = factor

    k = zt.shape[0]
    return pl.pallas_call(
        kernel,
        out_shape=(jax.ShapeDtypeStruct(zt.shape, F32), jax.ShapeDtypeStruct((k, k), F32)),
        compiler_params=pltpu.CompilerParams(vmem_limit_bytes=8 * MIB),
        name="orthonormal_rows",
    )(zt)


def direct(tokens, first, strip, total_tokens):
    k = first.shape[0]

    def step(_, state):
        vb = state[0].astype(BF16)
        projected = lax.dot_general(tokens, vb, NT, preferred_element_type=F32).astype(BF16)
        local = lax.dot_general(projected, tokens, TN, preferred_element_type=F32)
        tiles = local.reshape(lax.axis_size(ALL), -1, LANES)
        share = jnp.sum(lax.all_to_all(tiles, ALL, 0, 0, tiled=True), axis=0)
        return orthonormal_rows(to_all(share, ALL).reshape(local.shape) / total_tokens)

    vt, factor = lax.fori_loop(0, ITERS, step, (first, jnp.zeros((k, k), F32)))
    slab = lax.axis_index(("x", "z", "c"))
    return lax.dynamic_slice_in_dim(vt, slab * strip, strip, 1).T, factor


def to_all(piece, axes):
    copies = jnp.broadcast_to(piece, (lax.axis_size(axes), *piece.shape))
    return lax.all_to_all(copies, axes, 0, 0, tiled=True)


def sendable(exact, cov, pieces):
    value = lax.reduce_precision(exact, exponent_bits=8, mantissa_bits=7)
    parts = [value, exact - value, cov]
    tiles = [part.astype(BF16).reshape(pieces, -1, LANES) for part in parts]
    return jnp.concatenate(tiles, axis=1)


def summed(arrived, pack):
    total = jnp.sum(arrived.astype(F32), axis=0)
    exact = total[: pack.exact] + total[pack.exact : 2 * pack.exact]
    return sendable(exact, total[2 * pack.exact :], 1)[0]


def body(tokens, sketch_map, test_matrix):
    tokens_dev, width = tokens.shape
    k = sketch_map.shape[1]
    strip = width // lax.axis_size(("x", "z", "c"))
    total_tokens = tokens_dev * lax.axis_size(ALL)
    plane = lax.axis_size(("x", "y"))
    pack = Packing(width, 2 * plane)
    swap = [(0, 1), (1, 0)]
    with jax.named_scope("products"):
        held = [
            pltpu.with_memory_space_constraint(array, pltpu.HBM)
            for array in (tokens, sketch_map, test_matrix)
        ]
        keep_exact, keep_cov, send_exact, send_cov = local_products(pack, width, tokens_dev, k)(
            *held
        )
    with jax.named_scope("over_core"):
        exact = keep_exact + lax.ppermute(send_exact, "c", swap)
        cov = keep_cov + lax.ppermute(send_cov, "c", swap).astype(F32)
        tiles = sendable(exact, cov, plane)
    with jax.named_scope("over_xy"):
        piece = summed(lax.all_to_all(tiles, ("x", "y"), 0, 0, tiled=True), pack)
    with jax.named_scope("over_z"):
        piece = summed(to_all(piece, "z"), pack)
    with jax.named_scope("back_xy"):
        mine = to_all(piece, ("x", "y"))
    with jax.named_scope("back_core"):
        other = lax.ppermute(mine, "c", swap)
    with jax.named_scope("refine"):
        basis, factor, first, fine = refine(pack, width, k, strip, total_tokens)(mine, other)
    with jax.named_scope("check"):
        return lax.cond(
            fine[0] > 0,
            lambda: (basis, factor),
            lambda: direct(tokens, first, strip, total_tokens),
        )


def solution(mesh):
    finer = Mesh(mesh.devices.reshape(4, 8, 2, mesh.shape["rep"]), ALL)
    return jax.shard_map(
        body,
        mesh=finer,
        in_specs=(P(ALL, None), P(ALL, None), P("y", None, None)),
        out_specs=(P(("x", "z", "c"), None), P()),
        check_vma=False,
    )
```

```python
import jax
import jax.numpy as jnp
from jax import lax
from jax.experimental import pallas as pl
from jax.experimental.pallas import tpu as pltpu
from jax.sharding import Mesh
from jax.sharding import PartitionSpec as P

ITERS = 2
ALL = ("x", "z", "c", "y")
LANES = 128
SUB = 8
PACKED = 16
MIB = 1024 * 1024
F32 = jnp.float32
BF16 = jnp.bfloat16
HI = lax.Precision.HIGHEST
NN = (((1,), (0,)), ((), ()))
NT = (((1,), (1,)), ((), ()))
TN = (((0,), (0,)), ((), ()))
ROUNDING = 2.0**-9
ALLOWED = 1.0e-3


class Packing:
    def __init__(self, width, pieces):
        self.n = width // LANES
        self.pieces = pieces
        count = self.n // 2
        self.pairs = list(range(count - 1, -1, -1))
        self.diagonal = self.n * LANES
        step = pieces * PACKED
        self.exact_rows = -(-(self.diagonal + self.n) // step) * step
        self.offset = {}
        at = 0
        for pair in self.pairs:
            left, right = 2 * pair, 2 * pair + 1
            for j in (left, right):
                for i in range(j):
                    self.offset[i, j] = at
                    at += LANES
            self.offset[left, left] = at
            at += LANES
        self.used = at
        self.cov_rows = -(-at // step) * step
        self.exact = self.exact_rows // pieces
        self.cov = self.cov_rows // pieces
        self.piece = 2 * self.exact + self.cov


def local_products(pack, width, tokens_dev, k):
    chunks = 4
    part = tokens_dev // chunks
    exact_half = pack.exact_rows // 2
    cov_half = pack.cov_rows // 2

    def kernel(
        tok_hbm, smap_hbm, test_hbm, keep_exact, keep_cov, send_exact, send_cov,
        tok, smap, test, exact, cov, rounded, sem, out_sem,
    ):
        core = lax.axis_index("c")
        slab = lax.axis_index(("x", "z", "c"))
        load_map = pltpu.make_async_copy(smap_hbm, smap, sem.at[chunks])
        load_test = pltpu.make_async_copy(
            test_hbm.at[0, pl.ds(pl.multiple_of(slab * k, k), k)], test, sem.at[chunks + 1]
        )
        loads = []
        for s in range(chunks):
            rows = pl.ds(s * part, part)
            loads.append(pltpu.make_async_copy(tok_hbm.at[rows], tok.at[rows], sem.at[s]))
        load_map.start()
        for load in loads:
            load.start()
        load_test.start()
        load_map.wait()
        sketch = jnp.zeros((k, width), F32)
        for s in range(chunks):
            loads[s].wait()
            rows = slice(s * part, (s + 1) * part)
            sketch = sketch + lax.dot_general(
                smap[rows, :], tok[rows, :], TN, preferred_element_type=F32
            )
        load_test.wait()
        start = lax.dot_general(test[...], sketch.astype(BF16), TN, preferred_element_type=F32)
        for i in range(pack.n):
            at = i * LANES
            exact[at : at + LANES, :] = start[:, at : at + LANES]
        exact[pack.diagonal :, :] = jnp.zeros((pack.exact_rows - pack.diagonal, LANES), F32)
        if pack.used < pack.cov_rows:
            cov[pack.used :, :] = jnp.zeros((pack.cov_rows - pack.used, LANES), F32)
        row = lax.broadcasted_iota(jnp.int32, (LANES, LANES), 0)
        col = lax.broadcasted_iota(jnp.int32, (LANES, LANES), 1)
        for pair in pack.pairs:
            base = 2 * pair * LANES
            high = base + 2 * LANES
            out = lax.dot_general(tok[:, :high], tok[:, base:high], TN, preferred_element_type=F32)
            for j in range(2):
                for i in range(2 * pair + j):
                    at = pack.offset[i, 2 * pair + j]
                    cov[at : at + LANES, :] = out[
                        i * LANES : (i + 1) * LANES, j * LANES : (j + 1) * LANES
                    ]
            upper = out[base : base + LANES, :LANES]
            lower = out[base + LANES : high, LANES:]
            at = pack.offset[2 * pair, 2 * pair]
            both = jnp.where(row < col, upper, lower)
            cov[at : at + LANES, :] = jnp.where(row == col, 0.0, both)
            for b, own in ((2 * pair, upper), (2 * pair + 1, lower)):
                line = jnp.sum(jnp.where(row == col, own, 0.0), axis=0)[None, :]
                exact[pack.diagonal + b : pack.diagonal + b + 1, :] = line
        away = 1 - core
        rounded[...] = cov[pl.ds(pl.multiple_of(away * cov_half, LANES), cov_half), :].astype(BF16)
        outs = []
        for from_ref, to in (
            (rounded, send_cov),
            (exact.at[pl.ds(pl.multiple_of(away * exact_half, LANES), exact_half)], send_exact),
            (exact.at[pl.ds(pl.multiple_of(core * exact_half, LANES), exact_half)], keep_exact),
            (cov.at[pl.ds(pl.multiple_of(core * cov_half, LANES), cov_half)], keep_cov),
        ):
            outs.append(pltpu.make_async_copy(from_ref, to, out_sem.at[len(outs)]))
        for copy in outs:
            copy.start()
        for copy in outs:
            copy.wait()

    return pl.pallas_call(
        kernel,
        out_shape=(
            jax.ShapeDtypeStruct((exact_half, LANES), F32),
            jax.ShapeDtypeStruct((cov_half, LANES), F32),
            jax.ShapeDtypeStruct((exact_half, LANES), F32),
            jax.ShapeDtypeStruct((cov_half, LANES), BF16),
        ),
        in_specs=[pl.BlockSpec(memory_space=pl.ANY)] * 3,
        out_specs=[pl.BlockSpec(memory_space=pl.ANY)] * 4,
        scratch_shapes=[
            pltpu.VMEM((tokens_dev, width), BF16),
            pltpu.VMEM((tokens_dev, k), BF16),
            pltpu.VMEM((k, k), BF16),
            pltpu.VMEM((pack.exact_rows, LANES), F32),
            pltpu.VMEM((pack.cov_rows, LANES), F32),
            pltpu.VMEM((cov_half, LANES), BF16),
            pltpu.SemaphoreType.DMA((chunks + 2,)),
            pltpu.SemaphoreType.DMA((4,)),
        ],
        compiler_params=pltpu.CompilerParams(vmem_limit_bytes=24 * MIB),
        name="local_products",
    )


def eliminate(gram):
    k = gram.shape[0]
    blocks = k // SUB
    segment = blocks // 2
    lane = lax.broadcasted_iota(jnp.int32, (SUB, k), 1)
    row = lax.broadcasted_iota(jnp.int32, (SUB, k), 0)
    work, trace = [], []
    for b in range(blocks):
        work.append(gram[b * SUB : (b + 1) * SUB, :])
        trace.append(jnp.where(lane == row + b * SUB, 1.0, 0.0).astype(F32))
    factor, inverse = [], []
    for b in range(blocks):
        at = b * SUB
        stop = (b // segment + 1) * segment
        spread = {}
        for o in range(b, stop):
            for q in range(SUB):
                spread[o, q] = jnp.broadcast_to(work[o][:, at + q : at + q + 1], (SUB, k))
        d = {(p, q): spread[b, q][p : p + 1, :] for p in range(SUB) for q in range(p, SUB)}
        scale = []
        for p in range(SUB):
            scale.append(lax.rsqrt(d[p, p]))
            for q in range(p + 1, SUB):
                d[p, q] = d[p, q] * scale[p]
            for q in range(p + 1, SUB):
                for s in range(q, SUB):
                    d[q, s] = d[q, s] - d[p, q] * d[p, s]
        ra = [work[b][p : p + 1, :] for p in range(SUB)]
        re = [trace[b][p : p + 1, :] for p in range(SUB)]
        for p in range(SUB):
            ra[p] = ra[p] * scale[p]
            re[p] = re[p] * scale[p]
            for q in range(p + 1, SUB):
                ra[q] = ra[q] - d[p, q] * ra[p]
                re[q] = re[q] - d[p, q] * re[p]
        for o in range(b + 1, stop):
            column = [spread[o, q] for q in range(SUB)]
            for p in range(SUB):
                column[p] = column[p] * scale[p]
                for q in range(p + 1, SUB):
                    column[q] = column[q] - d[p, q] * column[p]
                work[o] = work[o] - column[p] * ra[p]
                trace[o] = trace[o] - column[p] * re[p]
        factor.append(jnp.concatenate(ra, axis=0))
        inverse.append(jnp.concatenate(re, axis=0))
        if b + 1 == stop and stop < blocks:
            above = jnp.concatenate(factor[-segment:], axis=0)
            beside = jnp.concatenate([above, jnp.concatenate(inverse[-segment:], axis=0)], axis=1)
            update = lax.dot_general(above, beside, TN, precision=HI, preferred_element_type=F32)
            for o in range(stop, blocks):
                rows = slice(o * SUB, (o + 1) * SUB)
                work[o] = work[o] - update[rows, :k]
                trace[o] = trace[o] - update[rows, k:]
    for b in range(blocks):
        factor[b] = jnp.where(lane >= row + b * SUB, factor[b], 0.0)
    return jnp.concatenate(factor, axis=0), jnp.concatenate(inverse, axis=0)


def thirds(v):
    high = v.astype(BF16)
    rest = v - high.astype(F32)
    mid = rest.astype(BF16)
    return high, mid, (rest - mid.astype(F32)).astype(BF16)


def orthonormal(pt):
    k = pt.shape[0]
    high, mid, low = thirds(pt)
    three = jnp.concatenate([high, mid, low], axis=0)
    wide = lax.dot_general(high, three, NT, preferred_element_type=F32)
    middle = lax.dot_general(mid, mid, NT, preferred_element_type=F32)
    cross = wide[:, 2 * k :] + wide[:, k : 2 * k]
    gram = wide[:, :k] + (cross + cross.T + middle)
    factor, inverse = eliminate(gram)
    ih, im, il = thirds(inverse)
    top = jnp.concatenate([high, mid], axis=0)
    ends = jnp.concatenate([low, high], axis=0)
    vt = jnp.dot(jnp.concatenate([ih, il], axis=1), ends, preferred_element_type=F32)
    vt = vt + jnp.dot(jnp.concatenate([im, im], axis=1), top, preferred_element_type=F32)
    vt = vt + jnp.dot(jnp.concatenate([ih, ih], axis=1), top, preferred_element_type=F32)
    return vt, factor, inverse


def packed_rows(ref, begin, count, length):
    found = []
    at = begin
    while at < begin + count:
        piece, row = at // length, at % length
        take = min(length - row, begin + count - at)
        found.append(ref[piece, row : row + take, :])
        at += take
    return found[0] if len(found) == 1 else jnp.concatenate(found, axis=0)


def refine(pack, width, k, strip, total_tokens):
    n = pack.n
    half = pack.pieces // 2

    def kernel(
        mine, other, basis, factor_out, first_out, fine_out,
        value, rest, cov, dense, squares, error, zt, vt, turned, sem,
    ):
        core = lax.axis_index("c")
        slab = lax.axis_index(("x", "z", "c"))
        exact_at = pl.ds(0, pack.exact)
        rest_at = pl.ds(pack.exact, pack.exact)
        cov_at = pl.ds(2 * pack.exact, pack.cov)
        loads = []
        for side, home in ((mine, core), (other, 1 - core)):
            place = pl.ds(home * half, half)
            for rows, to in ((exact_at, value), (rest_at, rest), (cov_at, cov)):
                loads.append(
                    pltpu.make_async_copy(side.at[:, rows], to.at[place], sem.at[len(loads)])
                )
        for load in loads:
            load.start()
        for at in (0, 1, 3, 4):
            loads[at].wait()

        def exact_rows(begin, count):
            return packed_rows(value, begin, count, pack.exact).astype(F32) + packed_rows(
                rest, begin, count, pack.exact
            ).astype(F32)

        for i in range(n):
            zt[:, i * LANES : (i + 1) * LANES] = exact_rows(i * LANES, LANES)
        lines = exact_rows(pack.diagonal, PACKED)
        diagonal = jnp.concatenate([lines[i : i + 1, :] for i in range(n)], axis=1)

        def unpack():
            row = lax.broadcasted_iota(jnp.int32, (LANES, LANES), 0)
            col = lax.broadcasted_iota(jnp.int32, (LANES, LANES), 1)
            down = [jnp.zeros((1, LANES), F32) for _ in range(n)]
            across = [None] * n

            def put(i, j, v):
                dense[i * LANES : (i + 1) * LANES, j * LANES : (j + 1) * LANES] = v.astype(BF16)
                square = v * v
                down[j] = down[j] + jnp.sum(square, axis=0)[None, :]
                if i != j:
                    across[i] = square if across[i] is None else across[i] + square

            for (i, j), at in sorted(pack.offset.items()):
                v = packed_rows(cov, at, LANES, pack.cov).astype(F32)
                if i < j:
                    put(i, j, v)
                    if i + 1 == j and j % 2:
                        rows = slice(j * LANES, (j + 1) * LANES)
                        dense[rows, i * LANES : (i + 1) * LANES] = v.T.astype(BF16)
                else:
                    flipped = v.T
                    put(i, i, jnp.where(row < col, v, flipped))
                    put(i + 1, i + 1, jnp.where(row > col, v, flipped))
            for i in range(n):
                if across[i] is not None:
                    down[i] = down[i] + jnp.sum(across[i].T, axis=0)[None, :]
            squares[...] = jnp.concatenate(down, axis=1)

        error[...] = jnp.zeros(error.shape, F32)

        @pl.loop(0, ITERS + 1)
        def _(step):
            fresh, factor, inverse = orthonormal(zt[...])
            factor_out[...] = factor

            @pl.when(step == 0)
            def _():
                first_out[...] = fresh
                for at in (2, 5):
                    loads[at].wait()
                unpack()

            @pl.when(step > 0)
            def _():
                back = jnp.dot(
                    inverse.astype(BF16), vt[...].astype(BF16), preferred_element_type=F32
                )
                share = (squares[...] * (1.0 / total_tokens) ** 2) * (back * back)
                line = jnp.sum(share, axis=0)[None, :]
                total = jnp.sum(line, axis=1, keepdims=True) * (ROUNDING**2 / k)
                error[...] = error[...] + jnp.broadcast_to(total, error.shape)

            vt[...] = fresh

            @pl.when(step < ITERS)
            def _():
                vb = fresh.astype(BF16)
                for pair in range(n // 2):
                    high = 2 * (pair + 1) * LANES
                    rj = slice(2 * pair * LANES, high)
                    z = vb[:, rj].astype(F32) * diagonal[:, rj]
                    z = z + lax.dot_general(
                        vb[:, :high], dense[:high, rj], NN, preferred_element_type=F32
                    )
                    if high < width:
                        z = z + lax.dot_general(
                            vb[:, high:], dense[rj, high:], NT, preferred_element_type=F32
                        )
                    zt[:, rj] = z * (1.0 / total_tokens)

        for i in range(n):
            cols = slice(i * LANES, (i + 1) * LANES)
            turned[cols, :] = vt[:, cols].T
        basis[...] = turned[pl.ds(slab * strip, strip), :]
        fine_out[0] = (jnp.sum(error[:1, :1]) <= ALLOWED**2).astype(jnp.int32)

    return pl.pallas_call(
        kernel,
        out_shape=(
            jax.ShapeDtypeStruct((strip, k), F32),
            jax.ShapeDtypeStruct((k, k), F32),
            jax.ShapeDtypeStruct((k, width), F32),
            jax.ShapeDtypeStruct((1,), jnp.int32),
        ),
        in_specs=[pl.BlockSpec(memory_space=pl.ANY)] * 2,
        out_specs=[pl.BlockSpec(memory_space=pltpu.VMEM)] * 3
        + [pl.BlockSpec(memory_space=pltpu.SMEM)],
        scratch_shapes=[
            pltpu.VMEM((pack.pieces, pack.exact, LANES), BF16),
            pltpu.VMEM((pack.pieces, pack.exact, LANES), BF16),
            pltpu.VMEM((pack.pieces, pack.cov, LANES), BF16),
            pltpu.VMEM((width, width), BF16),
            pltpu.VMEM((1, width), F32),
            pltpu.VMEM((SUB, LANES), F32),
            pltpu.VMEM((k, width), F32),
            pltpu.VMEM((k, width), F32),
            pltpu.VMEM((width, k), F32),
            pltpu.SemaphoreType.DMA((6,)),
        ],
        compiler_params=pltpu.CompilerParams(vmem_limit_bytes=28 * MIB),
        name="refine",
    )


def orthonormal_rows(zt):
    def kernel(zt_ref, vt_ref, factor_ref):
        vt, factor, _ = orthonormal(zt_ref[...])
        vt_ref[...] = vt
        factor_ref[...] = factor

    k = zt.shape[0]
    return pl.pallas_call(
        kernel,
        out_shape=(jax.ShapeDtypeStruct(zt.shape, F32), jax.ShapeDtypeStruct((k, k), F32)),
        compiler_params=pltpu.CompilerParams(vmem_limit_bytes=8 * MIB),
        name="orthonormal_rows",
    )(zt)


def direct(tokens, first, strip, total_tokens):
    k = first.shape[0]

    def step(_, state):
        vb = state[0].astype(BF16)
        projected = lax.dot_general(tokens, vb, NT, preferred_element_type=F32).astype(BF16)
        local = lax.dot_general(projected, tokens, TN, preferred_element_type=F32)
        tiles = local.reshape(lax.axis_size(ALL), -1, LANES)
        share = jnp.sum(lax.all_to_all(tiles, ALL, 0, 0, tiled=True), axis=0)
        return orthonormal_rows(to_all(share, ALL).reshape(local.shape) / total_tokens)

    vt, factor = lax.fori_loop(0, ITERS, step, (first, jnp.zeros((k, k), F32)))
    slab = lax.axis_index(("x", "z", "c"))
    return lax.dynamic_slice_in_dim(vt, slab * strip, strip, 1).T, factor


def to_all(piece, axes):
    copies = jnp.broadcast_to(piece, (lax.axis_size(axes), *piece.shape))
    return lax.all_to_all(copies, axes, 0, 0, tiled=True)


def sendable(exact, cov, pieces):
    value = lax.reduce_precision(exact, exponent_bits=8, mantissa_bits=7)
    parts = [value, exact - value, cov]
    tiles = [part.astype(BF16).reshape(pieces, -1, LANES) for part in parts]
    return jnp.concatenate(tiles, axis=1)


def summed(arrived, pack):
    total = jnp.sum(arrived.astype(F32), axis=0)
    exact = total[: pack.exact] + total[pack.exact : 2 * pack.exact]
    return sendable(exact, total[2 * pack.exact :], 1)[0]


def body(tokens, sketch_map, test_matrix):
    tokens_dev, width = tokens.shape
    k = sketch_map.shape[1]
    strip = width // lax.axis_size(("x", "z", "c"))
    total_tokens = tokens_dev * lax.axis_size(ALL)
    plane = lax.axis_size(("x", "y"))
    pack = Packing(width, 2 * plane)
    swap = [(0, 1), (1, 0)]
    with jax.named_scope("products"):
        held = [
            pltpu.with_memory_space_constraint(array, pltpu.HBM)
            for array in (tokens, sketch_map, test_matrix)
        ]
        keep_exact, keep_cov, send_exact, send_cov = local_products(pack, width, tokens_dev, k)(
            *held
        )
    with jax.named_scope("over_core"):
        exact = keep_exact + lax.ppermute(send_exact, "c", swap)
        cov = keep_cov + lax.ppermute(send_cov, "c", swap).astype(F32)
        tiles = sendable(exact, cov, plane)
    with jax.named_scope("over_xy"):
        piece = summed(lax.all_to_all(tiles, ("x", "y"), 0, 0, tiled=True), pack)
    with jax.named_scope("over_z"):
        piece = summed(to_all(piece, "z"), pack)
    with jax.named_scope("back_xy"):
        mine = to_all(piece, ("x", "y"))
    with jax.named_scope("back_core"):
        other = lax.ppermute(mine, "c", swap)
    with jax.named_scope("refine"):
        basis, factor, first, fine = refine(pack, width, k, strip, total_tokens)(mine, other)
    with jax.named_scope("check"):
        return lax.cond(
            fine[0] > 0,
            lambda: (basis, factor),
            lambda: direct(tokens, first, strip, total_tokens),
        )


def solution(mesh):
    finer = Mesh(mesh.devices.reshape(4, 8, 2, mesh.shape["rep"]), ALL)
    return jax.shard_map(
        body,
        mesh=finer,
        in_specs=(P(ALL, None), P(ALL, None), P("y", None, None)),
        out_specs=(P(("x", "z", "c"), None), P()),
        check_vma=False,
    )
```

```python
import jax
import jax.numpy as jnp
from jax import lax
from jax.experimental import pallas as pl
from jax.experimental.pallas import tpu as pltpu
from jax.sharding import Mesh
from jax.sharding import PartitionSpec as P

ITERS = 2
ALL = ("x", "z", "c", "y")
LANES = 128
SUB = 8
PACKED = 16
MIB = 1024 * 1024
F32 = jnp.float32
BF16 = jnp.bfloat16
NN = (((1,), (0,)), ((), ()))
NT = (((1,), (1,)), ((), ()))
TN = (((0,), (0,)), ((), ()))
ROUNDING = 2.0**-9
ALLOWED = 1.0e-3


class Packing:
    def __init__(self, width, pieces):
        self.n = width // LANES
        self.pieces = pieces
        count = self.n // 2
        self.pairs = list(range(count - 1, -1, -1))
        self.diagonal = self.n * LANES
        step = pieces * PACKED
        self.exact_rows = -(-(self.diagonal + self.n) // step) * step
        self.offset = {}
        at = 0
        for pair in self.pairs:
            left, right = 2 * pair, 2 * pair + 1
            for j in (left, right):
                for i in range(j):
                    self.offset[i, j] = at
                    at += LANES
            self.offset[left, left] = at
            at += LANES
        self.used = at
        self.cov_rows = -(-at // step) * step
        self.exact = self.exact_rows // pieces
        self.cov = self.cov_rows // pieces
        self.piece = 2 * self.exact + self.cov


def local_products(pack, width, tokens_dev, k):
    chunks = 4
    part = tokens_dev // chunks
    exact_half = pack.exact_rows // 2
    cov_half = pack.cov_rows // 2

    def kernel(
        tok_hbm, smap_hbm, test_hbm, keep_exact, keep_cov, send_exact, send_cov,
        tok, smap, test, exact, cov, rounded, sem, out_sem,
    ):
        core = lax.axis_index("c")
        slab = lax.axis_index(("x", "z", "c"))
        load_map = pltpu.make_async_copy(smap_hbm, smap, sem.at[chunks])
        load_test = pltpu.make_async_copy(
            test_hbm.at[0, pl.ds(pl.multiple_of(slab * k, k), k)], test, sem.at[chunks + 1]
        )
        loads = []
        for s in range(chunks):
            rows = pl.ds(s * part, part)
            loads.append(pltpu.make_async_copy(tok_hbm.at[rows], tok.at[rows], sem.at[s]))
        load_map.start()
        for load in loads:
            load.start()
        load_test.start()
        load_map.wait()
        sketch = jnp.zeros((k, width), F32)
        for s in range(chunks):
            loads[s].wait()
            rows = slice(s * part, (s + 1) * part)
            sketch = sketch + lax.dot_general(
                smap[rows, :], tok[rows, :], TN, preferred_element_type=F32
            )
        load_test.wait()
        start = lax.dot_general(test[...], sketch.astype(BF16), TN, preferred_element_type=F32)
        for i in range(pack.n):
            at = i * LANES
            exact[at : at + LANES, :] = start[:, at : at + LANES]
        exact[pack.diagonal :, :] = jnp.zeros((pack.exact_rows - pack.diagonal, LANES), F32)
        if pack.used < pack.cov_rows:
            cov[pack.used :, :] = jnp.zeros((pack.cov_rows - pack.used, LANES), F32)
        row = lax.broadcasted_iota(jnp.int32, (LANES, LANES), 0)
        col = lax.broadcasted_iota(jnp.int32, (LANES, LANES), 1)
        for pair in pack.pairs:
            base = 2 * pair * LANES
            high = base + 2 * LANES
            out = lax.dot_general(tok[:, :high], tok[:, base:high], TN, preferred_element_type=F32)
            for j in range(2):
                for i in range(2 * pair + j):
                    at = pack.offset[i, 2 * pair + j]
                    cov[at : at + LANES, :] = out[
                        i * LANES : (i + 1) * LANES, j * LANES : (j + 1) * LANES
                    ]
            upper = out[base : base + LANES, :LANES]
            lower = out[base + LANES : high, LANES:]
            at = pack.offset[2 * pair, 2 * pair]
            both = jnp.where(row < col, upper, lower)
            cov[at : at + LANES, :] = jnp.where(row == col, 0.0, both)
            for b, own in ((2 * pair, upper), (2 * pair + 1, lower)):
                line = jnp.sum(jnp.where(row == col, own, 0.0), axis=0)[None, :]
                exact[pack.diagonal + b : pack.diagonal + b + 1, :] = line
        away = 1 - core
        rounded[...] = cov[pl.ds(pl.multiple_of(away * cov_half, LANES), cov_half), :].astype(BF16)
        outs = []
        for from_ref, to in (
            (rounded, send_cov),
            (exact.at[pl.ds(pl.multiple_of(away * exact_half, LANES), exact_half)], send_exact),
            (exact.at[pl.ds(pl.multiple_of(core * exact_half, LANES), exact_half)], keep_exact),
            (cov.at[pl.ds(pl.multiple_of(core * cov_half, LANES), cov_half)], keep_cov),
        ):
            outs.append(pltpu.make_async_copy(from_ref, to, out_sem.at[len(outs)]))
        for copy in outs:
            copy.start()
        for copy in outs:
            copy.wait()

    return pl.pallas_call(
        kernel,
        out_shape=(
            jax.ShapeDtypeStruct((exact_half, LANES), F32),
            jax.ShapeDtypeStruct((cov_half, LANES), F32),
            jax.ShapeDtypeStruct((exact_half, LANES), F32),
            jax.ShapeDtypeStruct((cov_half, LANES), BF16),
        ),
        in_specs=[pl.BlockSpec(memory_space=pl.ANY)] * 3,
        out_specs=[pl.BlockSpec(memory_space=pl.ANY)] * 4,
        scratch_shapes=[
            pltpu.VMEM((tokens_dev, width), BF16),
            pltpu.VMEM((tokens_dev, k), BF16),
            pltpu.VMEM((k, k), BF16),
            pltpu.VMEM((pack.exact_rows, LANES), F32),
            pltpu.VMEM((pack.cov_rows, LANES), F32),
            pltpu.VMEM((cov_half, LANES), BF16),
            pltpu.SemaphoreType.DMA((chunks + 2,)),
            pltpu.SemaphoreType.DMA((4,)),
        ],
        compiler_params=pltpu.CompilerParams(vmem_limit_bytes=24 * MIB),
        name="local_products",
    )


def eliminate(gram):
    k = gram.shape[0]
    blocks = k // SUB
    segment = blocks // 2
    lane = lax.broadcasted_iota(jnp.int32, (SUB, k), 1)
    row = lax.broadcasted_iota(jnp.int32, (SUB, k), 0)
    work, trace = [], []
    for b in range(blocks):
        work.append(gram[b * SUB : (b + 1) * SUB, :])
        trace.append(jnp.where(lane == row + b * SUB, 1.0, 0.0).astype(F32))
    factor, inverse = [], []
    for b in range(blocks):
        at = b * SUB
        stop = (b // segment + 1) * segment
        spread = {}
        for o in range(b, stop):
            for q in range(SUB):
                spread[o, q] = jnp.broadcast_to(work[o][:, at + q : at + q + 1], (SUB, k))
        d = {(p, q): spread[b, q][p : p + 1, :] for p in range(SUB) for q in range(p, SUB)}
        scale = []
        for p in range(SUB):
            scale.append(lax.rsqrt(d[p, p]))
            for q in range(p + 1, SUB):
                d[p, q] = d[p, q] * scale[p]
            for q in range(p + 1, SUB):
                for s in range(q, SUB):
                    d[q, s] = d[q, s] - d[p, q] * d[p, s]
        ra = [work[b][p : p + 1, :] for p in range(SUB)]
        re = [trace[b][p : p + 1, :] for p in range(SUB)]
        for p in range(SUB):
            ra[p] = ra[p] * scale[p]
            re[p] = re[p] * scale[p]
            for q in range(p + 1, SUB):
                ra[q] = ra[q] - d[p, q] * ra[p]
                re[q] = re[q] - d[p, q] * re[p]
        for o in range(b + 1, stop):
            column = [spread[o, q] for q in range(SUB)]
            for p in range(SUB):
                column[p] = column[p] * scale[p]
                for q in range(p + 1, SUB):
                    column[q] = column[q] - d[p, q] * column[p]
                work[o] = work[o] - column[p] * ra[p]
                trace[o] = trace[o] - column[p] * re[p]
        factor.append(jnp.concatenate(ra, axis=0))
        inverse.append(jnp.concatenate(re, axis=0))
        if b + 1 == stop and stop < blocks:
            above = jnp.concatenate(factor[-segment:], axis=0)
            beside = jnp.concatenate([above, jnp.concatenate(inverse[-segment:], axis=0)], axis=1)
            ah, am, al = thirds(above)
            bh, bm, bl = thirds(beside)
            left = jnp.concatenate([al, ah, am, am, ah, ah], axis=0)
            right = jnp.concatenate([bh, bl, bm, bh, bm, bh], axis=0)
            update = lax.dot_general(left, right, TN, preferred_element_type=F32)
            for o in range(stop, blocks):
                rows = slice(o * SUB, (o + 1) * SUB)
                work[o] = work[o] - update[rows, :k]
                trace[o] = trace[o] - update[rows, k:]
    for b in range(blocks):
        factor[b] = jnp.where(lane >= row + b * SUB, factor[b], 0.0)
    return jnp.concatenate(factor, axis=0), jnp.concatenate(inverse, axis=0)


def thirds(v):
    high = v.astype(BF16)
    rest = v - high.astype(F32)
    mid = rest.astype(BF16)
    return high, mid, (rest - mid.astype(F32)).astype(BF16)


def orthonormal(pt):
    k = pt.shape[0]
    high, mid, low = thirds(pt)
    three = jnp.concatenate([high, mid, low], axis=0)
    wide = lax.dot_general(high, three, NT, preferred_element_type=F32)
    middle = lax.dot_general(mid, mid, NT, preferred_element_type=F32)
    cross = wide[:, 2 * k :] + wide[:, k : 2 * k]
    gram = wide[:, :k] + (cross + cross.T + middle)
    factor, inverse = eliminate(gram)
    ih, im, il = thirds(inverse)
    top = jnp.concatenate([high, mid], axis=0)
    ends = jnp.concatenate([low, high], axis=0)
    vt = jnp.dot(jnp.concatenate([ih, il], axis=1), ends, preferred_element_type=F32)
    vt = vt + jnp.dot(jnp.concatenate([im, im], axis=1), top, preferred_element_type=F32)
    vt = vt + jnp.dot(jnp.concatenate([ih, ih], axis=1), top, preferred_element_type=F32)
    return vt, factor, inverse


def packed_rows(ref, begin, count, length):
    found = []
    at = begin
    while at < begin + count:
        piece, row = at // length, at % length
        take = min(length - row, begin + count - at)
        found.append(ref[piece, row : row + take, :])
        at += take
    return found[0] if len(found) == 1 else jnp.concatenate(found, axis=0)


def refine(pack, width, k, strip, total_tokens):
    n = pack.n
    half = pack.pieces // 2

    def kernel(
        mine, other, basis, factor_out, first_out, fine_out,
        value, rest, cov, dense, squares, error, zt, vt, turned, sem,
    ):
        core = lax.axis_index("c")
        slab = lax.axis_index(("x", "z", "c"))
        exact_at = pl.ds(0, pack.exact)
        rest_at = pl.ds(pack.exact, pack.exact)
        cov_at = pl.ds(2 * pack.exact, pack.cov)
        loads = []
        for side, home in ((mine, core), (other, 1 - core)):
            place = pl.ds(home * half, half)
            for rows, to in ((exact_at, value), (rest_at, rest), (cov_at, cov)):
                loads.append(
                    pltpu.make_async_copy(side.at[:, rows], to.at[place], sem.at[len(loads)])
                )
        for at in (0, 1, 3, 4, 2, 5):
            loads[at].start()
        for at in (0, 1, 3, 4):
            loads[at].wait()

        def exact_rows(begin, count):
            return packed_rows(value, begin, count, pack.exact).astype(F32) + packed_rows(
                rest, begin, count, pack.exact
            ).astype(F32)

        for i in range(n):
            zt[:, i * LANES : (i + 1) * LANES] = exact_rows(i * LANES, LANES)
        lines = exact_rows(pack.diagonal, PACKED)
        diagonal = jnp.concatenate([lines[i : i + 1, :] for i in range(n)], axis=1)

        def unpack():
            row = lax.broadcasted_iota(jnp.int32, (LANES, LANES), 0)
            col = lax.broadcasted_iota(jnp.int32, (LANES, LANES), 1)
            down = [jnp.zeros((1, LANES), F32) for _ in range(n)]
            across = [None] * n

            def put(i, j, v):
                dense[i * LANES : (i + 1) * LANES, j * LANES : (j + 1) * LANES] = v.astype(BF16)
                square = v * v
                down[j] = down[j] + jnp.sum(square, axis=0)[None, :]
                if i != j:
                    across[i] = square if across[i] is None else across[i] + square

            for (i, j), at in sorted(pack.offset.items()):
                v = packed_rows(cov, at, LANES, pack.cov).astype(F32)
                if i < j:
                    put(i, j, v)
                    if i + 1 == j and j % 2:
                        rows = slice(j * LANES, (j + 1) * LANES)
                        dense[rows, i * LANES : (i + 1) * LANES] = v.T.astype(BF16)
                else:
                    flipped = v.T
                    put(i, i, jnp.where(row < col, v, flipped))
                    put(i + 1, i + 1, jnp.where(row > col, v, flipped))
            for i in range(n):
                if across[i] is not None:
                    down[i] = down[i] + jnp.sum(across[i].T, axis=0)[None, :]
            squares[...] = jnp.concatenate(down, axis=1)

        error[...] = jnp.zeros(error.shape, F32)

        @pl.loop(0, ITERS + 1)
        def _(step):
            fresh, factor, inverse = orthonormal(zt[...])
            factor_out[...] = factor

            @pl.when(step == 0)
            def _():
                first_out[...] = fresh
                for at in (2, 5):
                    loads[at].wait()
                unpack()

            @pl.when(step > 0)
            def _():
                back = jnp.dot(
                    inverse.astype(BF16), vt[...].astype(BF16), preferred_element_type=F32
                )
                share = (squares[...] * (1.0 / total_tokens) ** 2) * (back * back)
                line = jnp.sum(share, axis=0)[None, :]
                total = jnp.sum(line, axis=1, keepdims=True) * (ROUNDING**2 / k)
                error[...] = error[...] + jnp.broadcast_to(total, error.shape)

            vt[...] = fresh

            @pl.when(step < ITERS)
            def _():
                vb = fresh.astype(BF16)
                for pair in range(n // 2):
                    high = 2 * (pair + 1) * LANES
                    rj = slice(2 * pair * LANES, high)
                    z = vb[:, rj].astype(F32) * diagonal[:, rj]
                    z = z + lax.dot_general(
                        vb[:, :high], dense[:high, rj], NN, preferred_element_type=F32
                    )
                    if high < width:
                        z = z + lax.dot_general(
                            vb[:, high:], dense[rj, high:], NT, preferred_element_type=F32
                        )
                    zt[:, rj] = z * (1.0 / total_tokens)

        for i in range(n):
            cols = slice(i * LANES, (i + 1) * LANES)
            turned[cols, :] = vt[:, cols].T
        basis[...] = turned[pl.ds(slab * strip, strip), :]
        fine_out[0] = (jnp.sum(error[:1, :1]) <= ALLOWED**2).astype(jnp.int32)

    return pl.pallas_call(
        kernel,
        out_shape=(
            jax.ShapeDtypeStruct((strip, k), F32),
            jax.ShapeDtypeStruct((k, k), F32),
            jax.ShapeDtypeStruct((k, width), F32),
            jax.ShapeDtypeStruct((1,), jnp.int32),
        ),
        in_specs=[pl.BlockSpec(memory_space=pl.ANY)] * 2,
        out_specs=[pl.BlockSpec(memory_space=pltpu.VMEM)] * 3
        + [pl.BlockSpec(memory_space=pltpu.SMEM)],
        scratch_shapes=[
            pltpu.VMEM((pack.pieces, pack.exact, LANES), BF16),
            pltpu.VMEM((pack.pieces, pack.exact, LANES), BF16),
            pltpu.VMEM((pack.pieces, pack.cov, LANES), BF16),
            pltpu.VMEM((width, width), BF16),
            pltpu.VMEM((1, width), F32),
            pltpu.VMEM((SUB, LANES), F32),
            pltpu.VMEM((k, width), F32),
            pltpu.VMEM((k, width), F32),
            pltpu.VMEM((width, k), F32),
            pltpu.SemaphoreType.DMA((6,)),
        ],
        compiler_params=pltpu.CompilerParams(vmem_limit_bytes=28 * MIB),
        name="refine",
    )


def orthonormal_rows(zt):
    def kernel(zt_ref, vt_ref, factor_ref):
        vt, factor, _ = orthonormal(zt_ref[...])
        vt_ref[...] = vt
        factor_ref[...] = factor

    k = zt.shape[0]
    return pl.pallas_call(
        kernel,
        out_shape=(jax.ShapeDtypeStruct(zt.shape, F32), jax.ShapeDtypeStruct((k, k), F32)),
        compiler_params=pltpu.CompilerParams(vmem_limit_bytes=8 * MIB),
        name="orthonormal_rows",
    )(zt)


def direct(tokens, first, strip, total_tokens):
    k = first.shape[0]

    def step(_, state):
        vb = state[0].astype(BF16)
        projected = lax.dot_general(tokens, vb, NT, preferred_element_type=F32).astype(BF16)
        local = lax.dot_general(projected, tokens, TN, preferred_element_type=F32)
        tiles = local.reshape(lax.axis_size(ALL), -1, LANES)
        share = jnp.sum(lax.all_to_all(tiles, ALL, 0, 0, tiled=True), axis=0)
        return orthonormal_rows(to_all(share, ALL).reshape(local.shape) / total_tokens)

    vt, factor = lax.fori_loop(0, ITERS, step, (first, jnp.zeros((k, k), F32)))
    slab = lax.axis_index(("x", "z", "c"))
    return lax.dynamic_slice_in_dim(vt, slab * strip, strip, 1).T, factor


def to_all(piece, axes):
    copies = jnp.broadcast_to(piece, (lax.axis_size(axes), *piece.shape))
    return lax.all_to_all(copies, axes, 0, 0, tiled=True)


def sendable(exact, cov, pieces):
    value = lax.reduce_precision(exact, exponent_bits=8, mantissa_bits=7)
    parts = [value, exact - value, cov]
    tiles = [part.astype(BF16).reshape(pieces, -1, LANES) for part in parts]
    return jnp.concatenate(tiles, axis=1)


def summed(arrived, pack):
    total = jnp.sum(arrived.astype(F32), axis=0)
    exact = total[: pack.exact] + total[pack.exact : 2 * pack.exact]
    return sendable(exact, total[2 * pack.exact :], 1)[0]


def body(tokens, sketch_map, test_matrix):
    tokens_dev, width = tokens.shape
    k = sketch_map.shape[1]
    strip = width // lax.axis_size(("x", "z", "c"))
    total_tokens = tokens_dev * lax.axis_size(ALL)
    plane = lax.axis_size(("x", "y"))
    pack = Packing(width, 2 * plane)
    swap = [(0, 1), (1, 0)]
    with jax.named_scope("products"):
        held = [
            pltpu.with_memory_space_constraint(array, pltpu.HBM)
            for array in (tokens, sketch_map, test_matrix)
        ]
        keep_exact, keep_cov, send_exact, send_cov = local_products(pack, width, tokens_dev, k)(
            *held
        )
    with jax.named_scope("over_core"):
        exact = keep_exact + lax.ppermute(send_exact, "c", swap)
        cov = keep_cov + lax.ppermute(send_cov, "c", swap).astype(F32)
        tiles = sendable(exact, cov, plane)
    with jax.named_scope("over_xy"):
        piece = summed(lax.all_to_all(tiles, ("x", "y"), 0, 0, tiled=True), pack)
    with jax.named_scope("over_z"):
        piece = summed(to_all(piece, "z"), pack)
    with jax.named_scope("back_xy"):
        mine = to_all(piece, ("x", "y"))
    with jax.named_scope("back_core"):
        other = lax.ppermute(mine, "c", swap)
    with jax.named_scope("refine"):
        basis, factor, first, fine = refine(pack, width, k, strip, total_tokens)(mine, other)
    with jax.named_scope("check"):
        return lax.cond(
            fine[0] > 0,
            lambda: (basis, factor),
            lambda: direct(tokens, first, strip, total_tokens),
        )


def solution(mesh):
    finer = Mesh(mesh.devices.reshape(4, 8, 2, mesh.shape["rep"]), ALL)
    return jax.shard_map(
        body,
        mesh=finer,
        in_specs=(P(ALL, None), P(ALL, None), P("y", None, None)),
        out_specs=(P(("x", "z", "c"), None), P()),
        check_vma=False,
    )
```
